32 devices in a mesh: row: 16 (over z, y, x), col: 2 (over core).
Axes of the slice: x: 2, y: 2, z: 4, core: 2. Of those that a mesh axis runs over, the one named last changes fastest.
Arguments:
- flow_state: float32 [4, 128, 64, 1024], P(None, 'row', 'col'), may hold values from -6 to 6
- spacing: float32 [128], replicated, may hold values from 0.004 to 0.012
- diffusivity: float32 [4], replicated, may hold values from 0.03 to 0.1
Outputs:
- flow_next: float32 [4, 128, 64, 1024], P(None, 'row', 'col')
The draws below stay inside these ranges and needn't reach their ends.
All inputs are finite; a program needn't handle non-finite values.
Results may differ from the reference program's by a relative error of at most 0.00023.
Values sent between devices are 32-bit elements; how exact they have to be, the bound alone decides.
A program may use at most 128 MiB of HBM per device.

```python
import math
import jax
import jax.numpy as jnp
from jax import lax

NZ = 128
NX = 1024
NY = 64


def steps_of(own_key, shape, shards, least, largest):
    factor_of, own = 1.0, jax.random.fold_in(own_key, 6)
    for position, parts in shards:
        draws = jnp.exp(jax.random.uniform(jax.random.fold_in(own, position), (parts,), jnp.float32, least / len(shards), largest / len(shards)))
        factor_of = factor_of * jnp.repeat(draws, shape[position] // parts).reshape([-1 if axis == position else 1 for axis in range(len(shape))])
    return factor_of


def noise(key, extent, spread, limit, shards=(), kind=jnp.bfloat16):
    values = spread * jax.random.normal(key, extent, jnp.float32)
    if shards:
        values = values * steps_of(key, extent, shards, -0.22, 0.18)
    return jnp.clip(values, -limit, limit).astype(kind)


def setup_inputs(seed: int = 0) -> dict:
    key_of = jax.random.split(jax.random.key(seed), 4)
    flow_state = noise(key_of[0], (4, NZ, NY, NX), 1.0, 6.0, ((1, 16), (2, 2)), jnp.float32)
    spacing = jnp.clip(jnp.exp(jax.random.uniform(key_of[1], (NZ,), jnp.float32, math.log(0.004), math.log(0.012))), 0.004, 0.012)
    diffusivity = jnp.clip(jnp.exp(jax.random.uniform(key_of[2], (4,), jnp.float32, math.log(0.03), math.log(0.1))), 0.03, 0.1)
    return {"flow_state": flow_state, "spacing": spacing, "diffusivity": diffusivity}


time_step = 0.02
cell_width = 0.1
buoyancy = 1.0

def wall_geometry(spacing):
    centres = jnp.cumsum(spacing)
    positions = jnp.concatenate([centres[:1] - spacing[:1], centres, centres[-1:] + spacing[-1:]])
    gap_below = positions[1:-1] - positions[:-2]
    gap_above = positions[2:] - positions[1:-1]
    across = positions[2:] - positions[:-2]
    return (gap_below, gap_above, across)

def line_system(spacing, diffusivity):
    gap_below, gap_above, across = wall_geometry(spacing)
    diffuse_rate = time_step * diffusivity[:, None]
    lower_band = -2.0 * diffuse_rate / (across * gap_below)
    upper_band = -2.0 * diffuse_rate / (across * gap_above)
    middle = 1.0 - lower_band - upper_band
    levels = jnp.arange(spacing.shape[0])
    lower_band = jnp.where(levels == 0, 0.0, lower_band)
    upper_band = jnp.where(levels == spacing.shape[0] - 1, 0.0, upper_band)
    return (lower_band, middle, upper_band)

def advance(centre, speeds, z_down, z_up, y_left, y_right, across, diffusivity, forcing):
    x_left = jnp.roll(centre, 1, axis=-1)
    x_right = jnp.roll(centre, -1, axis=-1)
    advection = speeds[0] * (x_right - x_left) / (2.0 * cell_width)
    advection = advection + speeds[1] * (y_right - y_left) / (2.0 * cell_width)
    advection = advection + speeds[2] * (z_up - z_down) / across[:, None, None]
    laplace = (x_right + x_left - 2.0 * centre) / cell_width ** 2
    laplace = laplace + (y_right + y_left - 2.0 * centre) / cell_width ** 2
    return centre + time_step * (diffusivity * laplace - advection + forcing)

def reference(flow_state, spacing, diffusivity):
    gap_below, gap_above, across = wall_geometry(spacing)
    lower_band, middle, upper_band = line_system(spacing, diffusivity)
    results = []
    for component in range(4):
        centre = flow_state[component]
        z_padded = jnp.pad(centre, ((1, 1), (0, 0), (0, 0)))
        if component == 2:
            forcing = buoyancy * flow_state[3]
        elif component == 3:
            forcing = flow_state[2]
        else:
            forcing = 0.0
        stepped = advance(centre, flow_state, z_padded[:-2], z_padded[2:], jnp.roll(centre, 1, axis=1), jnp.roll(centre, -1, axis=1), across, diffusivity[component], forcing)
        solved = lax.linalg.tridiagonal_solve(lower_band[component], middle[component], upper_band[component], stepped.reshape(stepped.shape[0], -1))
        results.append(solved.reshape(centre.shape))
    return jnp.stack(results)
```

```python
import functools

import jax
import jax.numpy as jnp
from jax import lax
from jax.experimental import pallas as pl
from jax.experimental.pallas import tpu as pltpu
from jax.sharding import PartitionSpec as P

time_step = 0.02
cell_width = 0.1
buoyancy = 1.0
UNROLL = 8
MESH = pl.DeviceIdType.MESH

LAM, RHO, MU, WIN, GEE, UPPER, QSH, DT_ACROSS, RATE, TABLES = range(10)


def moved(value, by):
    return pltpu.roll(value, by % value.shape[1], 1)


def pivots(low, upp, lane, sign):
    levels = low.shape[1]
    place = lane if sign == 1 else levels - 1 - lane
    one, zero = jnp.ones_like(low), jnp.zeros_like(low)
    before = jnp.where(place == 0, one, moved(upp, sign))
    a, b, c, d = one + low, before, one, before
    shift = 1
    while shift < levels:
        inside = place >= shift
        pa = jnp.where(inside, moved(a, sign * shift), one)
        pb = jnp.where(inside, moved(b, sign * shift), zero)
        pc = jnp.where(inside, moved(c, sign * shift), zero)
        pd = jnp.where(inside, moved(d, sign * shift), one)
        na, nb = a * pa + b * pc, a * pb + b * pd
        nc, nd = c * pa + d * pc, c * pb + d * pd
        scale = 1.0 / na
        a, b, c, d = na * scale, nb * scale, nc * scale, nd * scale
        shift *= 2
    g = a / c
    rho = 1.0 / (g + upp)
    return g, rho, g * rho, place


def fill_tables(width, thick, diff, tab):
    levels = thick.shape[1]
    lane = lax.broadcasted_iota(jnp.int32, (8, levels), 1)
    sub = lax.broadcasted_iota(jnp.int32, (8, levels), 0)
    comps = diff.shape[0]
    rate = jnp.zeros((8, levels), jnp.float32)
    for c in range(comps):
        rate = jnp.where(sub % comps == c, (2.0 * time_step) * diff[c], rate)
    below = jnp.broadcast_to(thick[...], (8, levels))
    above = jnp.where(lane == levels - 1, below, moved(below, -1))
    across = below + above
    low = rate / (across * below)
    upp = rate / (across * above)
    tables = {}
    for sign, first, second in ((1, low, upp), (-1, upp, low)):
        g, rho, ratio, place = pivots(first, second, lane, sign)
        lam = jnp.where(place == 0, 0.0, first * moved(rho, sign))
        window = lam
        for step in range(1, width):
            window = window * moved(lam, sign * step)
        ahead = jnp.where(place == 0, 1.0, moved(ratio, sign))
        tables[sign] = (lam, rho, second * rho, window, g, second, ahead)
    for index in range(QSH + 1):
        tab[index] = jnp.where(sub < comps, tables[1][index], tables[-1][index])
    tab[DT_ACROSS] = time_step / across
    tab[RATE] = rate


def step_kernel(
    rows, cols, group, state, spacing, diffusivity, out, q, thick, diff, vtab, tab, ysend, yrecv,
    wrecv, ploc, dup, tot, be, got, top, ztop, ret, pq, load, small, ysem, wsem, s1, s2, s3,
):
    comps, depth, ny, nx = q.shape
    levels = rows * depth
    count = rows // group
    piece = nx // group
    me, col = lax.axis_index("row"), lax.axis_index("col")
    z, g = me // group, me % group
    base = me * depth
    nxt, prv = (col + 1) % cols, (col + cols - 1) % cols

    loads = [
        pltpu.make_async_copy(state.at[c], q.at[c], load.at[c]) for c in range(comps)
    ]
    takes = [
        pltpu.make_async_copy(spacing, thick, small.at[0]),
        pltpu.make_async_copy(diffusivity, diff, small.at[1]),
    ]
    for copy in loads + takes:
        copy.start()

    barrier = pltpu.get_barrier_semaphore()
    for o in range(1, rows):
        pl.semaphore_signal(
            barrier, inc=1, device_id=((me + o) % rows, col), device_id_type=MESH
        )
    sides = [nxt] if cols == 2 else [nxt, prv]
    for side in sides:
        pl.semaphore_signal(barrier, inc=1, device_id=(me, side), device_id_type=MESH)
    def remote(src, dst, sems, index, device):
        return pltpu.make_async_remote_copy(
            src_ref=src,
            dst_ref=dst,
            send_sem=sems.at[(0, *index)],
            recv_sem=sems.at[(1, *index)],
            device_id=device,
            device_id_type=MESH,
        )

    w_down = remote(
        state.at[2, 0], wrecv.at[1], wsem, (1,), (jnp.maximum(me - 1, 0), col)
    )
    w_up = remote(
        state.at[2, depth - 1], wrecv.at[0], wsem, (0,), (jnp.minimum(me + 1, rows - 1), col)
    )

    for copy in takes:
        copy.wait()
    fill_tables(depth, thick, diff, vtab)
    publish = pltpu.make_async_copy(vtab, tab, small.at[2])
    publish.start()

    def y_copies(c):
        return [
            remote(ysend.at[c, 0], yrecv.at[c, 0], ysem, (c, 0), (me, nxt)),
            remote(ysend.at[c, 1], yrecv.at[c, 1], ysem, (c, 1), (me, prv)),
        ]

    for c in range(comps):
        loads[c].wait()
        for k in range(depth):
            ysend[c, 0, k : k + 1, :] = q[c, k, ny - 1 : ny, :]
            ysend[c, 1, k : k + 1, :] = q[c, k, 0:1, :]

    pl.semaphore_wait(barrier, rows - 1 + len(sides))

    @pl.when(me > 0)
    def _():
        w_down.start()

    @pl.when(me < rows - 1)
    def _():
        w_up.start()

    for c in range(comps):
        for copy in y_copies(c):
            copy.start()

    @pl.when(me == 0)
    def _():
        wrecv[0] = jnp.zeros((ny, nx), jnp.float32)

    @pl.when(me == rows - 1)
    def _():
        wrecv[1] = jnp.zeros((ny, nx), jnp.float32)

    def up(table, c, level):
        return tab[table, c, jnp.clip(level, 0, levels - 1)]

    def down(table, c, level):
        return tab[table, comps + c, jnp.clip(level, 0, levels - 1)]

    publish.wait()
    slab = 8
    row_of = lax.broadcasted_iota(jnp.int32, (slab, nx), 0)
    half = time_step / (2.0 * cell_width)

    def peer(o):
        return (g + o) % group

    def push(c, o):
        to = peer(o)
        return remote(
            be.at[c, to], got.at[c, o], s1, (c, o), (z * group + to, col)
        )

    def send_z(c, o, way):
        to = z + o if way == 0 else z - o
        to = jnp.clip(to, 0, count - 1)
        return remote(
            top.at[c, way], ztop.at[c, way, o - 1], s2, (c, way, o - 1), (to * group + g, col)
        )

    def give(c, o):
        to = peer(o)
        return remote(
            ret.at[c, to], pq.at[c, g], s3, (c, o), (z * group + to, col)
        )

    def stencil(c):
        for copy in y_copies(c):
            copy.wait_recv()
        alpha = tab[RATE, c, 0] * (0.5 / cell_width**2)
        keep = 1.0 - 4.0 * alpha
        for r in range(0, ny, slab):

            def level(k, carry, c=c, r=r, alpha=alpha, keep=keep):
                below, total, beta = carry
                scale = up(DT_ACROSS, 0, base + k)
                c_up = jnp.where(k == depth - 1, 0.0, scale)
                c_dn = jnp.where(k == 0, 0.0, scale)
                here = pl.ds(r, slab)
                centre = q[c, k, here, :]
                x_left = pltpu.roll(centre, 1, 1)
                x_right = pltpu.roll(centre, nx - 1, 1)
                if r == 0:
                    first = yrecv[c, 0, pl.ds(k, 1), :]
                else:
                    first = q[c, k, r - 1 : r, :]
                if r + slab == ny:
                    last = yrecv[c, 1, pl.ds(k, 1), :]
                else:
                    last = q[c, k, r + slab : r + slab + 1, :]
                y_left = jnp.where(row_of == 0, first, pltpu.roll(centre, 1, 0))
                y_right = jnp.where(row_of == slab - 1, last, pltpu.roll(centre, slab - 1, 0))
                z_up = q[c, jnp.minimum(k + 1, depth - 1), here, :]
                z_dn = q[c, jnp.maximum(k - 1, 0), here, :]
                value = keep * centre + alpha * ((x_left + x_right) + (y_left + y_right))
                value = value - (half * q[0, k, here, :]) * (x_right - x_left)
                value = value - (half * q[1, k, here, :]) * (y_right - y_left)
                value = value - q[2, k, here, :] * (c_up * z_up - c_dn * z_dn)
                if c == 2:
                    value = value + (time_step * buoyancy) * q[3, k, here, :]
                if c == 3:
                    value = value + time_step * q[2, k, here, :]
                below = value + up(LAM, c, base + k) * below
                out[c, k, here, :] = below
                total = total + beta * value
                return below, total, beta * down(LAM, c, base + k)

            start = jnp.zeros((slab, nx), jnp.float32)
            _, total, _ = lax.fori_loop(
                0, depth, level, (start, start, down(LAM, c, base - 1)), unroll=min(depth, UNROLL)
            )
            tot[c, pl.ds(r, slab), :] = total

    def finish(c):
        beta = down(LAM, c, base - 1)
        for k in range(depth):
            beta = beta * down(LAM, c, base + k)
        pi = 1.0
        for k in range(1, depth):
            pi = pi * up(LAM, c, base + k)
        for r in range(0, ny, slab):
            here = pl.ds(r, slab)
            below, total = out[c, depth - 1, here, :], tot[c, here, :]
            d_up = up(DT_ACROSS, 0, base + depth) * (wrecv[1, here, :] * q[c, depth - 1, here, :])
            d_dn = -up(DT_ACROSS, 0, base - 1) * (wrecv[0, here, :] * q[c, 0, here, :])
            p_loc = up(LAM, c, base) * d_dn
            ploc[c, here, :] = p_loc
            dup[c, here, :] = down(LAM, c, base + depth - 1) * d_up
            b = up(LAM, c, base + depth) * (below + pi * p_loc) + d_up
            e = total + beta * d_up + d_dn
            for p in range(group):
                be[c, p, 0, here, :] = b[:, p * piece : (p + 1) * piece]
                be[c, p, 1, here, :] = e[:, p * piece : (p + 1) * piece]
        for o in range(1, group):
            push(c, o).start()
        got[c, 0] = be[c, g]

    for c in range(comps):
        stencil(c)
        if c == 1:

            @pl.when(me > 0)
            def _():
                w_up.wait_recv()

            @pl.when(me < rows - 1)
            def _():
                w_down.wait_recv()

            finish(0)
        if c >= 1:
            finish(c)

    def up_factor(c, j):
        return up(WIN, c, (j + 1) * depth)

    def down_factor(c, j):
        return down(WIN, c, j * depth - 1)

    def slot(other):
        return (g + group - other) % group

    for c in range(comps):
        for o in range(1, group):
            push(c, o).wait_recv()
        total = got[c, slot(0), 0]
        for j in range(1, group):
            total = got[c, slot(j), 0] + up_factor(c, z * group + j) * total
        top[c, 0] = total
        total = got[c, slot(group - 1), 1]
        for j in reversed(range(group - 1)):
            total = got[c, slot(j), 1] + down_factor(c, z * group + j) * total
        top[c, 1] = total
        for o in range(1, count):

            @pl.when(z + o < count)
            def _(c=c, o=o):
                send_z(c, o, 0).start()

            @pl.when(z - o >= 0)
            def _(c=c, o=o):
                send_z(c, o, 1).start()

    for c in range(comps):
        for way in range(2):
            acc = ret.at[c, 0, way]
            acc[...] = jnp.zeros((ny, piece), jnp.float32)
            weight = 1.0
            for o in range(1, count):
                source = z - o if way == 0 else z + o

                @pl.when((source >= 0) & (source < count))
                def _(c=c, o=o, way=way, weight=weight, acc=acc):
                    send_z(c, o, way).wait_recv()
                    acc[...] += weight * ztop[c, way, o - 1]

                for j in range(group):
                    device = source * group + j
                    weight = weight * (up_factor if way == 0 else down_factor)(c, device)
        carry = ret[c, 0, 0]
        for j in range(group):
            ret[c, j, 0] = carry
            if j < group - 1:
                carry = got[c, slot(j), 0] + up_factor(c, z * group + j) * carry
        carry = ret[c, 0, 1]
        for j in reversed(range(group)):
            ret[c, j, 1] = carry
            if j > 0:
                carry = got[c, slot(j), 1] + down_factor(c, z * group + j) * carry
        for o in range(1, group):
            give(c, o).start()
        pq[c, g] = ret[c, g]

    for c in range(comps):
        for o in range(1, group):
            source = (g + group - o) % group
            remote(
                ret.at[c, source], pq.at[c, source], s3, (c, o), (z * group + source, col)
            ).wait_recv()
        pis = [jnp.float32(1.0)]
        for k in range(1, depth):
            pis.append(pis[-1] * up(LAM, c, base + k))
        end = base + depth - 1
        den = up(GEE, c, end) + up(UPPER, c, end) * down(QSH, c, end)
        for p in range(group):
            span = pl.ds(p * piece, piece)
            carry = pq[c, p, 0] + ploc[c, :, span]
            x = out[c, depth - 1, :, span] + pis[-1] * carry
            x = (x + (pq[c, p, 1] + dup[c, :, span])) / den
            out[c, depth - 1, :, span] = x
            for k in reversed(range(depth - 1)):
                rho = up(RHO, c, base + k)
                x = rho * out[c, k, :, span] + (rho * pis[k]) * carry + up(MU, c, base + k) * x
                out[c, k, :, span] = x

    for c in range(comps):
        for copy in y_copies(c):
            copy.wait_send()

    @pl.when(me > 0)
    def _():
        w_down.wait_send()

    @pl.when(me < rows - 1)
    def _():
        w_up.wait_send()

    for c in range(comps):
        for o in range(1, group):
            push(c, o).wait_send()
            give(c, o).wait_send()
        for o in range(1, count):

            @pl.when(z + o < count)
            def _(c=c, o=o):
                send_z(c, o, 0).wait_send()

            @pl.when(z - o >= 0)
            def _(c=c, o=o):
                send_z(c, o, 1).wait_send()


def group_of(rows, nx):
    group = 1
    while group * group < rows and rows % (2 * group) == 0 and nx % (256 * group) == 0:
        group *= 2
    return group


def shards(rows, cols, flow_state, spacing, diffusivity):
    comps, depth, ny, nx = flow_state.shape
    group = group_of(rows, nx)
    count = rows // group
    piece = nx // group
    levels = spacing.shape[0]
    f32 = jnp.float32
    vmem = functools.partial(pltpu.VMEM, dtype=f32)
    dma = pltpu.SemaphoreType.DMA
    return pl.pallas_call(
        functools.partial(step_kernel, rows, cols, group),
        out_shape=jax.ShapeDtypeStruct(flow_state.shape, f32),
        in_specs=[pl.BlockSpec(memory_space=pltpu.HBM)] * 3,
        out_specs=pl.BlockSpec(memory_space=pltpu.VMEM),
        scratch_shapes=[
            vmem(flow_state.shape),
            vmem((1, levels)),
            pltpu.SMEM((comps,), f32),
            vmem((TABLES, 8, levels)),
            pltpu.SMEM((TABLES, 8, levels), f32),
            vmem((comps, 2, depth, nx)),
            vmem((comps, 2, depth, nx)),
            vmem((2, ny, nx)),
            vmem((comps, ny, nx)),
            vmem((comps, ny, nx)),
            vmem((comps, ny, nx)),
            vmem((comps, group, 2, ny, piece)),
            vmem((comps, group, 2, ny, piece)),
            vmem((comps, 2, ny, piece)),
            vmem((comps, 2, count - 1, ny, piece)),
            vmem((comps, group, 2, ny, piece)),
            vmem((comps, group, 2, ny, piece)),
            dma((comps,)),
            dma((3,)),
            dma((2, comps, 2)),
            dma((2, 2)),
            dma((2, comps, group)),
            dma((2, comps, 2, count - 1)),
            dma((2, comps, group)),
        ],
        compiler_params=pltpu.CompilerParams(
            collective_id=0, has_side_effects=True, vmem_limit_bytes=46 << 20
        ),
        name="convection_step",
    )(flow_state, pltpu.with_memory_space_constraint(spacing.reshape(1, levels), pltpu.HBM), pltpu.with_memory_space_constraint(diffusivity, pltpu.HBM))


def solution(mesh):
    rows, cols = mesh.shape["row"], mesh.shape["col"]
    placed = (P(None, "row", "col", None), P(), P())
    return jax.shard_map(
        functools.partial(shards, rows, cols),
        mesh=mesh,
        in_specs=placed,
        out_specs=P(None, "row", "col", None),
        check_vma=False,
    )
```

```python
import functools

import jax
import jax.numpy as jnp
from jax import lax
from jax.experimental import pallas as pl
from jax.experimental.pallas import tpu as pltpu
from jax.sharding import PartitionSpec as P

time_step = 0.02
cell_width = 0.1
buoyancy = 1.0
UNROLL = 8
HALVES = 2
LAG = 6
MESH = pl.DeviceIdType.MESH

LAM, RHO, MU, WIN, GEE, UPPER, QSH, DT_ACROSS, RATE, TABLES = range(10)


def moved(value, by):
    return pltpu.roll(value, by % value.shape[1], 1)


def pivots(low, upp, lane, sign):
    levels = low.shape[1]
    place = lane if sign == 1 else levels - 1 - lane
    one, zero = jnp.ones_like(low), jnp.zeros_like(low)
    before = jnp.where(place == 0, one, moved(upp, sign))
    a, b, c, d = one + low, before, one, before
    shift = 1
    while shift < levels:
        inside = place >= shift
        pa = jnp.where(inside, moved(a, sign * shift), one)
        pb = jnp.where(inside, moved(b, sign * shift), zero)
        pc = jnp.where(inside, moved(c, sign * shift), zero)
        pd = jnp.where(inside, moved(d, sign * shift), one)
        na, nb = a * pa + b * pc, a * pb + b * pd
        nc, nd = c * pa + d * pc, c * pb + d * pd
        scale = 1.0 / na
        a, b, c, d = na * scale, nb * scale, nc * scale, nd * scale
        shift *= 2
    g = a / c
    rho = 1.0 / (g + upp)
    return g, rho, g * rho, place


def fill_tables(width, thick, diff, tab):
    levels = thick.shape[1]
    lane = lax.broadcasted_iota(jnp.int32, (8, levels), 1)
    sub = lax.broadcasted_iota(jnp.int32, (8, levels), 0)
    comps = diff.shape[0]
    rate = jnp.zeros((8, levels), jnp.float32)
    for c in range(comps):
        rate = jnp.where(sub % comps == c, (2.0 * time_step) * diff[c], rate)
    below = jnp.broadcast_to(thick[...], (8, levels))
    above = jnp.where(lane == levels - 1, below, moved(below, -1))
    across = below + above
    low = rate / (across * below)
    upp = rate / (across * above)
    tables = {}
    for sign, first, second in ((1, low, upp), (-1, upp, low)):
        g, rho, ratio, place = pivots(first, second, lane, sign)
        lam = jnp.where(place == 0, 0.0, first * moved(rho, sign))
        window = lam
        for step in range(1, width):
            window = window * moved(lam, sign * step)
        ahead = jnp.where(place == 0, 1.0, moved(ratio, sign))
        tables[sign] = (lam, rho, second * rho, window, g, second, ahead)
    for index in range(QSH + 1):
        tab[index] = jnp.where(sub < comps, tables[1][index], tables[-1][index])
    tab[DT_ACROSS] = time_step / across
    tab[RATE] = rate


def step_kernel(
    rows, cols, group, halves, state, spacing, diffusivity, out, q, thick, diff, vtab, tab, ysend,
    yrecv, wrecv, ploc, dup, tot, be, got, top, ztop, ret, pq, load, small, ready, ysem, wsem, s1,
    s2, s3,
):
    comps, depth, ny, nx = q.shape
    levels = rows * depth
    count = rows // group
    piece = nx // group
    part = ny // halves
    me, col = lax.axis_index("row"), lax.axis_index("col")
    z, g = me // group, me % group
    base = me * depth
    nxt, prv = (col + 1) % cols, (col + cols - 1) % cols
    chunks = [(c, h) for h in range(halves) for c in range(comps)]

    loads = [
        pltpu.make_async_copy(state.at[c], q.at[c], load.at[c]) for c in range(comps)
    ]
    takes = [
        pltpu.make_async_copy(spacing, thick, small.at[0]),
        pltpu.make_async_copy(diffusivity, diff, small.at[1]),
    ]
    for copy in takes + loads:
        copy.start()

    barrier = pltpu.get_barrier_semaphore()
    ready_z, ready_w, ready_c = group, group + count, group + count + 1

    def signal(sem, when, device):
        @pl.when(when)
        def _():
            pl.semaphore_signal(sem, inc=1, device_id=device, device_id_type=MESH)

    def await_ready(index, when):
        @pl.when(when)
        def _():
            pl.semaphore_wait(ready.at[index], 1)

    def peer(o):
        return (g + o) % group

    for o in range(1, group):
        signal(barrier, g + o < group, (z * group + peer(o), col))
    for o in range(1, count):
        signal(barrier, z + o < count, (jnp.minimum(z + o, count - 1) * group + g, col))
    signal(barrier, me < rows - 1, (jnp.minimum(me + 1, rows - 1), col))
    signal(barrier, col < cols - 1, (me, nxt))
    if cols > 2:
        signal(barrier, col == 0, (me, prv))

    earlier = g + z + jnp.minimum(me, 1) + jnp.minimum(col, 1)
    if cols > 2:
        earlier = earlier + col // (cols - 1)

    @pl.when(earlier > 0)
    def _():
        pl.semaphore_wait(barrier, earlier)

    signal(ready.at[ready_w], me > 0, (jnp.maximum(me - 1, 0), col))
    signal(ready.at[ready_c], col > 0, (me, prv))
    if cols > 2:
        signal(ready.at[ready_c + 1], col == cols - 1, (me, nxt))
    for o in range(1, group):
        signal(ready.at[group - o], g + o >= group, (z * group + peer(o), col))
    for o in range(1, count):
        signal(ready.at[ready_z + o], z - o >= 0, (jnp.maximum(z - o, 0) * group + g, col))

    def remote(src, dst, sems, index, device):
        return pltpu.make_async_remote_copy(
            src_ref=src,
            dst_ref=dst,
            send_sem=sems.at[(0, *index)],
            recv_sem=sems.at[(1, *index)],
            device_id=device,
            device_id_type=MESH,
        )

    def w_down(h):
        here = pl.ds(h * part, part)
        return remote(
            state.at[2, 0, here], wrecv.at[1, here], wsem, (1, h), (jnp.maximum(me - 1, 0), col)
        )

    def w_up(h):
        here = pl.ds(h * part, part)
        return remote(
            state.at[2, depth - 1, here],
            wrecv.at[0, here],
            wsem,
            (0, h),
            (jnp.minimum(me + 1, rows - 1), col),
        )

    for h in range(halves):

        @pl.when(me > 0)
        def _(h=h):
            w_down(h).start()

        if h == 0:
            await_ready(ready_w, me < rows - 1)

        @pl.when(me < rows - 1)
        def _(h=h):
            w_up(h).start()

    for copy in takes:
        copy.wait()
    fill_tables(depth, thick, diff, vtab)
    publish = pltpu.make_async_copy(vtab, tab, small.at[2])
    publish.start()

    def y_copies(c):
        return [
            remote(ysend.at[c, 0], yrecv.at[c, 0], ysem, (c, 0), (me, nxt)),
            remote(ysend.at[c, 1], yrecv.at[c, 1], ysem, (c, 1), (me, prv)),
        ]

    for c in range(comps):
        loads[c].wait()
        for k in range(depth):
            ysend[c, 0, k : k + 1, :] = q[c, k, ny - 1 : ny, :]
            ysend[c, 1, k : k + 1, :] = q[c, k, 0:1, :]

    await_ready(ready_c, col < cols - 1)
    if cols > 2:
        await_ready(ready_c + 1, col == 0)
    for c in range(comps):
        for copy in y_copies(c):
            copy.start()

    @pl.when(me == 0)
    def _():
        wrecv[0] = jnp.zeros((ny, nx), jnp.float32)

    @pl.when(me == rows - 1)
    def _():
        wrecv[1] = jnp.zeros((ny, nx), jnp.float32)

    def up(table, c, level):
        return tab[table, c, jnp.clip(level, 0, levels - 1)]

    def down(table, c, level):
        return tab[table, comps + c, jnp.clip(level, 0, levels - 1)]

    publish.wait()
    slab = 8
    row_of = lax.broadcasted_iota(jnp.int32, (slab, nx), 0)
    half = time_step / (2.0 * cell_width)

    def push(i, o):
        to = peer(o)
        return remote(
            be.at[i, to], got.at[i, o], s1, (i, o), (z * group + to, col)
        )

    def send_z(i, o, way):
        to = z + o if way == 0 else z - o
        to = jnp.clip(to, 0, count - 1)
        return remote(
            top.at[i, way], ztop.at[i, way, o - 1], s2, (i, way, o - 1), (to * group + g, col)
        )

    def give(i, o):
        to = peer(o)
        return remote(
            ret.at[i, to], pq.at[i, g], s3, (i, o), (z * group + to, col)
        )

    def given(i, o):
        source = peer(group - o)
        return remote(
            ret.at[i, source], pq.at[i, source], s3, (i, o), (z * group + source, col)
        )

    def stencil(c):
        for copy in y_copies(c):
            copy.wait_recv()
        alpha = tab[RATE, c, 0] * (0.5 / cell_width**2)
        keep = 1.0 - 4.0 * alpha
        for r in range(0, ny, slab):

            def level(k, carry, c=c, r=r, alpha=alpha, keep=keep):
                below, total, beta = carry
                scale = up(DT_ACROSS, 0, base + k)
                c_up = jnp.where(k == depth - 1, 0.0, scale)
                c_dn = jnp.where(k == 0, 0.0, scale)
                here = pl.ds(r, slab)
                centre = q[c, k, here, :]
                x_left = pltpu.roll(centre, 1, 1)
                x_right = pltpu.roll(centre, nx - 1, 1)
                if r == 0:
                    first = yrecv[c, 0, pl.ds(k, 1), :]
                else:
                    first = q[c, k, r - 1 : r, :]
                if r + slab == ny:
                    last = yrecv[c, 1, pl.ds(k, 1), :]
                else:
                    last = q[c, k, r + slab : r + slab + 1, :]
                y_left = jnp.where(row_of == 0, first, pltpu.roll(centre, 1, 0))
                y_right = jnp.where(row_of == slab - 1, last, pltpu.roll(centre, slab - 1, 0))
                z_up = q[c, jnp.minimum(k + 1, depth - 1), here, :]
                z_dn = q[c, jnp.maximum(k - 1, 0), here, :]
                value = keep * centre + alpha * ((x_left + x_right) + (y_left + y_right))
                value = value - (half * q[0, k, here, :]) * (x_right - x_left)
                value = value - (half * q[1, k, here, :]) * (y_right - y_left)
                value = value - q[2, k, here, :] * (c_up * z_up - c_dn * z_dn)
                if c == 2:
                    value = value + (time_step * buoyancy) * q[3, k, here, :]
                if c == 3:
                    value = value + time_step * q[2, k, here, :]
                below = value + up(LAM, c, base + k) * below
                out[c, k, here, :] = below
                total = total + beta * value
                return below, total, beta * down(LAM, c, base + k)

            start = jnp.zeros((slab, nx), jnp.float32)
            _, total, _ = lax.fori_loop(
                0, depth, level, (start, start, down(LAM, c, base - 1)), unroll=min(depth, UNROLL)
            )
            tot[c, pl.ds(r, slab), :] = total

    def await_w(h):
        @pl.when(me > 0)
        def _():
            w_up(h).wait_recv()

        @pl.when(me < rows - 1)
        def _():
            w_down(h).wait_recv()

    def finish(i):
        c, h = chunks[i]
        beta = down(LAM, c, base - 1)
        for k in range(depth):
            beta = beta * down(LAM, c, base + k)
        pi = 1.0
        for k in range(1, depth):
            pi = pi * up(LAM, c, base + k)
        for r in range(0, part, slab):
            here, local = pl.ds(h * part + r, slab), pl.ds(r, slab)
            below, total = out[c, depth - 1, here, :], tot[c, here, :]
            d_up = up(DT_ACROSS, 0, base + depth) * (wrecv[1, here, :] * q[c, depth - 1, here, :])
            d_dn = -up(DT_ACROSS, 0, base - 1) * (wrecv[0, here, :] * q[c, 0, here, :])
            p_loc = up(LAM, c, base) * d_dn
            ploc[c, here, :] = p_loc
            dup[c, here, :] = down(LAM, c, base + depth - 1) * d_up
            b = up(LAM, c, base + depth) * (below + pi * p_loc) + d_up
            e = total + beta * d_up + d_dn
            for p in range(group):
                be[i, p, 0, local, :] = b[:, p * piece : (p + 1) * piece]
                be[i, p, 1, local, :] = e[:, p * piece : (p + 1) * piece]
        for o in range(1, group):
            if i == 0:
                await_ready(o, g + o < group)
            push(i, o).start()
        got[i, 0] = be[i, g]

    for c in range(comps):
        stencil(c)
        if c == min(1, comps - 1):
            await_w(0)
            for i in range(c):
                finish(i)
        if c >= 1:
            finish(c)
    for i in range(comps, len(chunks)):
        if i % comps == 0:
            await_w(i // comps)
        finish(i)

    def up_factor(c, j):
        return up(WIN, c, (j + 1) * depth)

    def down_factor(c, j):
        return down(WIN, c, j * depth - 1)

    def slot(other):
        return (g + group - other) % group

    def gather(i):
        c = chunks[i][0]
        for o in range(1, group):
            push(i, o).wait_recv()
        total = got[i, slot(0), 0]
        for j in range(1, group):
            total = got[i, slot(j), 0] + up_factor(c, z * group + j) * total
        top[i, 0] = total
        total = got[i, slot(group - 1), 1]
        for j in reversed(range(group - 1)):
            total = got[i, slot(j), 1] + down_factor(c, z * group + j) * total
        top[i, 1] = total
        for o in range(1, count):
            if i == 0:
                await_ready(ready_z + o, z + o < count)

            @pl.when(z + o < count)
            def _(o=o):
                send_z(i, o, 0).start()

            @pl.when(z - o >= 0)
            def _(o=o):
                send_z(i, o, 1).start()

    def scatter(i):
        c = chunks[i][0]
        for way in range(2):
            acc = ret.at[i, 0, way]
            acc[...] = jnp.zeros((part, piece), jnp.float32)
            weight = 1.0
            for o in range(1, count):
                source = z - o if way == 0 else z + o

                @pl.when((source >= 0) & (source < count))
                def _(o=o, way=way, weight=weight, acc=acc):
                    send_z(i, o, way).wait_recv()
                    acc[...] += weight * ztop[i, way, o - 1]

                for j in range(group):
                    device = source * group + j
                    weight = weight * (up_factor if way == 0 else down_factor)(c, device)
        carry = ret[i, 0, 0]
        for j in range(group):
            ret[i, j, 0] = carry
            if j < group - 1:
                carry = got[i, slot(j), 0] + up_factor(c, z * group + j) * carry
        carry = ret[i, 0, 1]
        for j in reversed(range(group)):
            ret[i, j, 1] = carry
            if j > 0:
                carry = got[i, slot(j), 1] + down_factor(c, z * group + j) * carry
        for o in range(1, group):
            give(i, o).start()
        pq[i, g] = ret[i, g]

    def settle(i):
        c, h = chunks[i]
        here = pl.ds(h * part, part)
        pis = [jnp.float32(1.0)]
        for k in range(1, depth):
            pis.append(pis[-1] * up(LAM, c, base + k))
        end = base + depth - 1
        den = up(GEE, c, end) + up(UPPER, c, end) * down(QSH, c, end)
        for o in range(group):
            p = peer(group - o)
            if o:
                given(i, o).wait_recv()
            span = pl.ds(pl.multiple_of(p * piece, piece), piece)
            carry = pq[i, p, 0] + ploc[c, here, span]
            x = out[c, depth - 1, here, span] + pis[-1] * carry
            x = (x + (pq[i, p, 1] + dup[c, here, span])) / den
            out[c, depth - 1, here, span] = x
            for k in reversed(range(depth - 1)):
                rho = up(RHO, c, base + k)
                x = rho * out[c, k, here, span] + (rho * pis[k]) * carry + up(MU, c, base + k) * x
                out[c, k, here, span] = x

    total_chunks = len(chunks)
    for i in range(total_chunks):
        gather(i)
        if i >= LAG:
            scatter(i - LAG)
    for i in range(max(total_chunks - LAG, 0), total_chunks):
        scatter(i)
    for i in range(total_chunks):
        settle(i)

    for c in range(comps):
        for copy in y_copies(c):
            copy.wait_send()

    for h in range(halves):

        @pl.when(me > 0)
        def _(h=h):
            w_down(h).wait_send()

        @pl.when(me < rows - 1)
        def _(h=h):
            w_up(h).wait_send()

    for i in range(total_chunks):
        for o in range(1, group):
            push(i, o).wait_send()
            give(i, o).wait_send()
        for o in range(1, count):

            @pl.when(z + o < count)
            def _(i=i, o=o):
                send_z(i, o, 0).wait_send()

            @pl.when(z - o >= 0)
            def _(i=i, o=o):
                send_z(i, o, 1).wait_send()


def group_of(rows, nx):
    group = 1
    while group * group < rows and rows % (2 * group) == 0 and nx % (256 * group) == 0:
        group *= 2
    return group


def shards(rows, cols, flow_state, spacing, diffusivity):
    comps, depth, ny, nx = flow_state.shape
    group = group_of(rows, nx)
    count = rows // group
    piece = nx // group
    halves = HALVES if ny % (8 * HALVES) == 0 else 1
    part = ny // halves
    chunks = comps * halves
    levels = spacing.shape[0]
    f32 = jnp.float32
    vmem = functools.partial(pltpu.VMEM, dtype=f32)
    dma = pltpu.SemaphoreType.DMA
    spacing = pltpu.with_memory_space_constraint(spacing.reshape(1, levels), pltpu.HBM)
    diffusivity = pltpu.with_memory_space_constraint(diffusivity, pltpu.HBM)
    return pl.pallas_call(
        functools.partial(step_kernel, rows, cols, group, halves),
        out_shape=jax.ShapeDtypeStruct(flow_state.shape, f32),
        in_specs=[pl.BlockSpec(memory_space=pltpu.HBM)] * 3,
        out_specs=pl.BlockSpec(memory_space=pltpu.VMEM),
        scratch_shapes=[
            vmem(flow_state.shape),
            vmem((1, levels)),
            pltpu.SMEM((comps,), f32),
            vmem((TABLES, 8, levels)),
            pltpu.SMEM((TABLES, 8, levels), f32),
            vmem((comps, 2, depth, nx)),
            vmem((comps, 2, depth, nx)),
            vmem((2, ny, nx)),
            vmem((comps, ny, nx)),
            vmem((comps, ny, nx)),
            vmem((comps, ny, nx)),
            vmem((chunks, group, 2, part, piece)),
            vmem((chunks, group, 2, part, piece)),
            vmem((chunks, 2, part, piece)),
            vmem((chunks, 2, max(count - 1, 1), part, piece)),
            vmem((chunks, group, 2, part, piece)),
            vmem((chunks, group, 2, part, piece)),
            dma((comps,)),
            dma((3,)),
            pltpu.SemaphoreType.REGULAR((group + count + 3,)),
            dma((2, comps, 2)),
            dma((2, 2, halves)),
            dma((2, chunks, group)),
            dma((2, chunks, 2, max(count - 1, 1))),
            dma((2, chunks, group)),
        ],
        compiler_params=pltpu.CompilerParams(
            collective_id=0, has_side_effects=True, vmem_limit_bytes=46 << 20
        ),
        name="convection_step",
    )(flow_state, spacing, diffusivity)


def solution(mesh):
    rows, cols = mesh.shape["row"], mesh.shape["col"]
    placed = (P(None, "row", "col", None), P(), P())
    return jax.shard_map(
        functools.partial(shards, rows, cols),
        mesh=mesh,
        in_specs=placed,
        out_specs=P(None, "row", "col", None),
        check_vma=False,
    )
```

```python
import functools

import jax
import jax.numpy as jnp
from jax import lax
from jax.experimental import pallas as pl
from jax.experimental.pallas import tpu as pltpu
from jax.sharding import PartitionSpec as P

time_step = 0.02
cell_width = 0.1
buoyancy = 1.0
UNROLL = 8
HALVES = 2
LAG = 6
MESH = pl.DeviceIdType.MESH

PUSH, ALONG_Z, GIVE, Y_ROWS, W_UP, W_DOWN = range(6)
LAM, RHO, MU, WIN, GEE, UPPER, QSH, DT_ACROSS, RATE, TABLES = range(10)


def moved(value, by):
    return pltpu.roll(value, by % value.shape[1], 1)


def pivots(low, upp, lane, sign):
    levels = low.shape[1]
    place = lane if sign == 1 else levels - 1 - lane
    one, zero = jnp.ones_like(low), jnp.zeros_like(low)
    before = jnp.where(place == 0, one, moved(upp, sign))
    a, b, c, d = one + low, before, one, before
    shift = 1
    while shift < levels:
        inside = place >= shift
        pa = jnp.where(inside, moved(a, sign * shift), one)
        pb = jnp.where(inside, moved(b, sign * shift), zero)
        pc = jnp.where(inside, moved(c, sign * shift), zero)
        pd = jnp.where(inside, moved(d, sign * shift), one)
        na, nb = a * pa + b * pc, a * pb + b * pd
        nc, nd = c * pa + d * pc, c * pb + d * pd
        scale = 1.0 / na
        a, b, c, d = na * scale, nb * scale, nc * scale, nd * scale
        shift *= 2
    g = a / c
    rho = 1.0 / (g + upp)
    return g, rho, g * rho, place


def fill_tables(width, thick, diff, tab):
    levels = thick.shape[1]
    lane = lax.broadcasted_iota(jnp.int32, (8, levels), 1)
    sub = lax.broadcasted_iota(jnp.int32, (8, levels), 0)
    comps = diff.shape[0]
    rate = jnp.zeros((8, levels), jnp.float32)
    for c in range(comps):
        rate = jnp.where(sub % comps == c, (2.0 * time_step) * diff[c], rate)
    below = jnp.broadcast_to(thick[...], (8, levels))
    above = jnp.where(lane == levels - 1, below, moved(below, -1))
    across = below + above
    low = rate / (across * below)
    upp = rate / (across * above)
    tables = {}
    for sign, first, second in ((1, low, upp), (-1, upp, low)):
        g, rho, ratio, place = pivots(first, second, lane, sign)
        lam = jnp.where(place == 0, 0.0, first * moved(rho, sign))
        window = lam
        for step in range(1, width):
            window = window * moved(lam, sign * step)
        ahead = jnp.where(place == 0, 1.0, moved(ratio, sign))
        tables[sign] = (lam, rho, second * rho, window, g, second, ahead)
    for index in range(QSH + 1):
        tab[index] = jnp.where(sub < comps, tables[1][index], tables[-1][index])
    tab[DT_ACROSS] = time_step / across
    tab[RATE] = rate


def step_kernel(
    rows, cols, group, halves, state, spacing, diffusivity, out, q, thick, diff, vtab, tab, ysend,
    yrecv, wrecv, ploc, dup, tot, be, got, top, ztop, ret, pq, small, ready, sent, load, ysem, wsem,
    s1, s2, s3,
):
    comps, depth, ny, nx = q.shape
    levels = rows * depth
    count = rows // group
    piece = nx // group
    part = ny // halves
    me, col = lax.axis_index("row"), lax.axis_index("col")
    z, g = me // group, me % group
    base = me * depth
    nxt, prv = (col + 1) % cols, (col + cols - 1) % cols
    chunks = [(c, h) for h in range(halves) for c in range(comps)]

    loads = [pltpu.make_async_copy(state, q, load)]
    takes = [
        pltpu.make_async_copy(spacing, thick, small.at[0]),
        pltpu.make_async_copy(diffusivity, diff, small.at[1]),
    ]
    for copy in takes + loads:
        copy.start()

    barrier = pltpu.get_barrier_semaphore()

    def signal(sem, when, device):
        @pl.when(when)
        def _():
            pl.semaphore_signal(sem, inc=1, device_id=device, device_id_type=MESH)

    def greet(device):
        pl.semaphore_signal(barrier, inc=1, device_id=device, device_id_type=MESH)

    def await_ready(o, when):
        @pl.when(when)
        def _():
            pl.semaphore_wait(ready.at[o - 1], 1)

    def peer(o):
        return (g + o) % group

    signal(barrier, me > 0, (jnp.maximum(me - 1, 0), col))
    signal(barrier, me < rows - 1, (jnp.minimum(me + 1, rows - 1), col))
    for o in range(1, group):
        greet((z * group + peer(o), col))
    sides = [nxt] if cols == 2 else [nxt, prv]
    for side in sides:
        greet((me, side))
    for o in range(1, count):
        signal(barrier, z + o < count, (jnp.minimum(z + o, count - 1) * group + g, col))
    greetings = group - 1 + len(sides) + z
    greetings = greetings + jnp.minimum(me, 1) + jnp.minimum(rows - 1 - me, 1)

    pl.semaphore_wait(barrier, greetings)

    def remote(src, dst, kind, sem, device):
        return pltpu.make_async_remote_copy(
            src_ref=src,
            dst_ref=dst,
            send_sem=sent.at[kind],
            recv_sem=sem,
            device_id=device,
            device_id_type=MESH,
        )

    def await_bytes(ref, sem):
        pltpu.make_async_copy(ref, ref, sem).wait()

    def w_down(h):
        here = pl.ds(h * part, part)
        return remote(
            state.at[2, 0, here],
            wrecv.at[1, here],
            W_DOWN,
            wsem.at[1, h],
            (jnp.maximum(me - 1, 0), col),
        )

    def w_up(h):
        here = pl.ds(h * part, part)
        return remote(
            state.at[2, depth - 1, here],
            wrecv.at[0, here],
            W_UP,
            wsem.at[0, h],
            (jnp.minimum(me + 1, rows - 1), col),
        )

    for h in range(halves):

        @pl.when(me > 0)
        def _(h=h):
            w_down(h).start()

        @pl.when(me < rows - 1)
        def _(h=h):
            w_up(h).start()

    for o in range(1, count):
        signal(ready.at[o - 1], z - o >= 0, (jnp.maximum(z - o, 0) * group + g, col))

    for copy in takes:
        copy.wait()
    fill_tables(depth, thick, diff, vtab)
    publish = pltpu.make_async_copy(vtab, tab, small.at[2])
    publish.start()

    def y_copies(c):
        return [
            remote(ysend.at[c, 0], yrecv.at[c, 0], Y_ROWS, ysem, (me, nxt)),
            remote(ysend.at[c, 1], yrecv.at[c, 1], Y_ROWS, ysem, (me, prv)),
        ]

    loads[0].wait()
    for c in range(comps):
        for k in range(depth):
            ysend[c, 0, k : k + 1, :] = q[c, k, ny - 1 : ny, :]
            ysend[c, 1, k : k + 1, :] = q[c, k, 0:1, :]

    for c in range(comps):
        for copy in y_copies(c):
            copy.start()

    @pl.when(me == 0)
    def _():
        wrecv[0] = jnp.zeros((ny, nx), jnp.float32)

    @pl.when(me == rows - 1)
    def _():
        wrecv[1] = jnp.zeros((ny, nx), jnp.float32)

    def up(table, c, level):
        return tab[table, c, jnp.clip(level, 0, levels - 1)]

    def down(table, c, level):
        return tab[table, comps + c, jnp.clip(level, 0, levels - 1)]

    publish.wait()
    slab = 8
    row_of = lax.broadcasted_iota(jnp.int32, (slab, nx), 0)
    half = time_step / (2.0 * cell_width)

    def push(i, o):
        to = peer(o)
        return remote(be.at[i, to], got.at[i, o], PUSH, s1.at[i], (z * group + to, col))

    def send_z(i, o, way):
        to = z + o if way == 0 else z - o
        to = jnp.clip(to, 0, count - 1)
        return remote(
            top.at[i, way], ztop.at[i, z_slot(o, way)], ALONG_Z, s2.at[i], (to * group + g, col)
        )

    def z_slot(o, way):
        return count - o - 1 if way == 0 else o - 1

    def give(i, o):
        to = peer(o)
        return remote(ret.at[i, to], pq.at[i, group - o], GIVE, s3.at[i], (z * group + to, col))

    def stencil(c):
        alpha = tab[RATE, c, 0] * (0.5 / cell_width**2)
        keep = 1.0 - 4.0 * alpha
        for r in range(0, ny, slab):

            def level(k, carry, c=c, r=r, alpha=alpha, keep=keep):
                below, total, beta = carry
                scale = up(DT_ACROSS, 0, base + k)
                c_up = jnp.where(k == depth - 1, 0.0, scale)
                c_dn = jnp.where(k == 0, 0.0, scale)
                here = pl.ds(r, slab)
                centre = q[c, k, here, :]
                x_left = pltpu.roll(centre, 1, 1)
                x_right = pltpu.roll(centre, nx - 1, 1)
                if r == 0:
                    first = yrecv[c, 0, pl.ds(k, 1), :]
                else:
                    first = q[c, k, r - 1 : r, :]
                if r + slab == ny:
                    last = yrecv[c, 1, pl.ds(k, 1), :]
                else:
                    last = q[c, k, r + slab : r + slab + 1, :]
                y_left = jnp.where(row_of == 0, first, pltpu.roll(centre, 1, 0))
                y_right = jnp.where(row_of == slab - 1, last, pltpu.roll(centre, slab - 1, 0))
                z_up = q[c, jnp.minimum(k + 1, depth - 1), here, :]
                z_dn = q[c, jnp.maximum(k - 1, 0), here, :]
                value = keep * centre + alpha * ((x_left + x_right) + (y_left + y_right))
                value = value - (half * q[0, k, here, :]) * (x_right - x_left)
                value = value - (half * q[1, k, here, :]) * (y_right - y_left)
                value = value - q[2, k, here, :] * (c_up * z_up - c_dn * z_dn)
                if c == 2:
                    value = value + (time_step * buoyancy) * q[3, k, here, :]
                if c == 3:
                    value = value + time_step * q[2, k, here, :]
                below = value + up(LAM, c, base + k) * below
                out[c, k, here, :] = below
                total = total + beta * value
                return below, total, beta * down(LAM, c, base + k)

            start = jnp.zeros((slab, nx), jnp.float32)
            _, total, _ = lax.fori_loop(
                0, depth, level, (start, start, down(LAM, c, base - 1)), unroll=min(depth, UNROLL)
            )
            tot[c, pl.ds(r, slab), :] = total

    def await_w(h):
        @pl.when(me > 0)
        def _():
            w_up(h).wait_recv()

        @pl.when(me < rows - 1)
        def _():
            w_down(h).wait_recv()

    def finish(i):
        c, h = chunks[i]
        beta = down(LAM, c, base - 1)
        for k in range(depth):
            beta = beta * down(LAM, c, base + k)
        pi = 1.0
        for k in range(1, depth):
            pi = pi * up(LAM, c, base + k)
        for r in range(0, part, slab):
            here, local = pl.ds(h * part + r, slab), pl.ds(r, slab)
            below, total = out[c, depth - 1, here, :], tot[c, here, :]
            d_up = up(DT_ACROSS, 0, base + depth) * (wrecv[1, here, :] * q[c, depth - 1, here, :])
            d_dn = -up(DT_ACROSS, 0, base - 1) * (wrecv[0, here, :] * q[c, 0, here, :])
            p_loc = up(LAM, c, base) * d_dn
            ploc[c, here, :] = p_loc
            dup[c, here, :] = down(LAM, c, base + depth - 1) * d_up
            b = up(LAM, c, base + depth) * (below + pi * p_loc) + d_up
            e = total + beta * d_up + d_dn
            for p in range(group):
                be[i, p, 0, local, :] = b[:, p * piece : (p + 1) * piece]
                be[i, p, 1, local, :] = e[:, p * piece : (p + 1) * piece]
        for o in range(1, group):
            push(i, o).start()
        got[i, 0] = be[i, g]

    await_bytes(yrecv, ysem)
    for c in range(comps):
        stencil(c)
        if c == min(1, comps - 1):
            await_w(0)
            for i in range(c):
                finish(i)
        if c >= 1:
            finish(c)
    for i in range(comps, len(chunks)):
        if i % comps == 0:
            await_w(i // comps)
        finish(i)

    def up_factor(c, j):
        return up(WIN, c, (j + 1) * depth)

    def down_factor(c, j):
        return down(WIN, c, j * depth - 1)

    def slot(other):
        return (g + group - other) % group

    def gather(i):
        c = chunks[i][0]
        if group > 1:
            await_bytes(got.at[i, pl.ds(1, group - 1)], s1.at[i])
        total = got[i, slot(0), 0]
        for j in range(1, group):
            total = got[i, slot(j), 0] + up_factor(c, z * group + j) * total
        top[i, 0] = total
        total = got[i, slot(group - 1), 1]
        for j in reversed(range(group - 1)):
            total = got[i, slot(j), 1] + down_factor(c, z * group + j) * total
        top[i, 1] = total
        for o in range(1, count):
            if i == 0:
                await_ready(o, z + o < count)

            @pl.when(z + o < count)
            def _(o=o):
                send_z(i, o, 0).start()

            @pl.when(z - o >= 0)
            def _(o=o):
                send_z(i, o, 1).start()

    def scatter(i):
        c = chunks[i][0]
        if count > 1:
            await_bytes(ztop.at[i], s2.at[i])
        for way in range(2):
            acc = ret.at[i, 0, way]
            acc[...] = jnp.zeros((part, piece), jnp.float32)
            weight = 1.0
            for o in range(1, count):
                source = z - o if way == 0 else z + o

                @pl.when((source >= 0) & (source < count))
                def _(o=o, way=way, weight=weight, acc=acc):
                    acc[...] += weight * ztop[i, z_slot(o, way)]

                for j in range(group):
                    device = source * group + j
                    weight = weight * (up_factor if way == 0 else down_factor)(c, device)
        carry = ret[i, 0, 0]
        for j in range(group):
            ret[i, j, 0] = carry
            if j < group - 1:
                carry = got[i, slot(j), 0] + up_factor(c, z * group + j) * carry
        carry = ret[i, 0, 1]
        for j in reversed(range(group)):
            ret[i, j, 1] = carry
            if j > 0:
                carry = got[i, slot(j), 1] + down_factor(c, z * group + j) * carry
        for o in range(1, group):
            give(i, o).start()
        pq[i, 0] = ret[i, g]

    def settle(i):
        c, h = chunks[i]
        here = pl.ds(h * part, part)
        pis = [jnp.float32(1.0)]
        for k in range(1, depth):
            pis.append(pis[-1] * up(LAM, c, base + k))
        end = base + depth - 1
        den = up(GEE, c, end) + up(UPPER, c, end) * down(QSH, c, end)
        if group > 1:
            await_bytes(pq.at[i, pl.ds(1, group - 1)], s3.at[i])
        for o in range(group):
            p = peer(o)
            span = pl.ds(pl.multiple_of(p * piece, piece), piece)
            carry = pq[i, o, 0] + ploc[c, here, span]
            x = out[c, depth - 1, here, span] + pis[-1] * carry
            x = (x + (pq[i, o, 1] + dup[c, here, span])) / den
            out[c, depth - 1, here, span] = x
            for k in reversed(range(depth - 1)):
                rho = up(RHO, c, base + k)
                x = rho * out[c, k, here, span] + (rho * pis[k]) * carry + up(MU, c, base + k) * x
                out[c, k, here, span] = x

    total_chunks = len(chunks)
    for i in range(total_chunks):
        gather(i)
        if i >= LAG:
            scatter(i - LAG)
    for i in range(max(total_chunks - LAG, 0), total_chunks):
        scatter(i)
    for i in range(total_chunks):
        settle(i)

    await_bytes(ysend, sent.at[Y_ROWS])

    @pl.when(me > 0)
    def _():
        await_bytes(wrecv.at[0], sent.at[W_DOWN])

    @pl.when(me < rows - 1)
    def _():
        await_bytes(wrecv.at[0], sent.at[W_UP])

    if group > 1:
        await_bytes(be.at[:, pl.ds(1, group - 1)], sent.at[PUSH])
        await_bytes(ret.at[:, pl.ds(1, group - 1)], sent.at[GIVE])
    if count > 1:
        await_bytes(ztop, sent.at[ALONG_Z])


def group_of(rows, nx):
    group = 1
    while group * group < rows and rows % (2 * group) == 0 and nx % (256 * group) == 0:
        group *= 2
    return group


def shards(rows, cols, flow_state, spacing, diffusivity):
    comps, depth, ny, nx = flow_state.shape
    group = group_of(rows, nx)
    count = rows // group
    piece = nx // group
    halves = HALVES if ny % (8 * HALVES) == 0 else 1
    part = ny // halves
    chunks = comps * halves
    levels = spacing.shape[0]
    f32 = jnp.float32
    vmem = functools.partial(pltpu.VMEM, dtype=f32)
    dma = pltpu.SemaphoreType.DMA
    spacing = pltpu.with_memory_space_constraint(spacing.reshape(1, levels), pltpu.HBM)
    diffusivity = pltpu.with_memory_space_constraint(diffusivity, pltpu.HBM)
    return pl.pallas_call(
        functools.partial(step_kernel, rows, cols, group, halves),
        out_shape=jax.ShapeDtypeStruct(flow_state.shape, f32),
        in_specs=[pl.BlockSpec(memory_space=pltpu.HBM)] * 3,
        out_specs=pl.BlockSpec(memory_space=pltpu.VMEM),
        scratch_shapes=[
            vmem(flow_state.shape),
            vmem((1, levels)),
            pltpu.SMEM((comps,), f32),
            vmem((TABLES, 8, levels)),
            pltpu.SMEM((TABLES, 8, levels), f32),
            vmem((comps, 2, depth, nx)),
            vmem((comps, 2, depth, nx)),
            vmem((2, ny, nx)),
            vmem((comps, ny, nx)),
            vmem((comps, ny, nx)),
            vmem((comps, ny, nx)),
            vmem((chunks, group, 2, part, piece)),
            vmem((chunks, group, 2, part, piece)),
            vmem((chunks, 2, part, piece)),
            vmem((chunks, max(count - 1, 1), part, piece)),
            vmem((chunks, group, 2, part, piece)),
            vmem((chunks, group, 2, part, piece)),
            dma((3,)),
            pltpu.SemaphoreType.REGULAR((max(count - 1, 1),)),
            dma((6,)),
            dma,
            dma,
            dma((2, halves)),
            dma((chunks,)),
            dma((chunks,)),
            dma((chunks,)),
        ],
        compiler_params=pltpu.CompilerParams(
            collective_id=0, has_side_effects=True, vmem_limit_bytes=46 << 20
        ),
        name="convection_step",
    )(flow_state, spacing, diffusivity)


def solution(mesh):
    rows, cols = mesh.shape["row"], mesh.shape["col"]
    placed = (P(None, "row", "col", None), P(), P())
    return jax.shard_map(
        functools.partial(shards, rows, cols),
        mesh=mesh,
        in_specs=placed,
        out_specs=P(None, "row", "col", None),
        check_vma=False,
    )
```

```python
import functools

import jax
import jax.numpy as jnp
from jax import lax
from jax.experimental import pallas as pl
from jax.experimental.pallas import tpu as pltpu
from jax.sharding import PartitionSpec as P

time_step = 0.02
cell_width = 0.1
buoyancy = 1.0
UNROLL = 8
HALVES = 2
LAG = 3
MESH = pl.DeviceIdType.MESH

PUSH, ALONG_Z, GIVE, Y_ROWS, W_UP, W_DOWN = range(6)
LAM, RHO, MU, WIN, GEE, UPPER, QSH, DT_ACROSS, RATE, TABLES = range(10)


def moved(value, by):
    return pltpu.roll(value, by % value.shape[1], 1)


def pivots(low, upp, lane, sign):
    levels = low.shape[1]
    place = lane if sign == 1 else levels - 1 - lane
    one, zero = jnp.ones_like(low), jnp.zeros_like(low)
    before = jnp.where(place == 0, one, moved(upp, sign))
    a, b, c, d = one + low, before, one, before
    shift = 1
    while shift < levels:
        inside = place >= shift
        pa = jnp.where(inside, moved(a, sign * shift), one)
        pb = jnp.where(inside, moved(b, sign * shift), zero)
        pc = jnp.where(inside, moved(c, sign * shift), zero)
        pd = jnp.where(inside, moved(d, sign * shift), one)
        na, nb = a * pa + b * pc, a * pb + b * pd
        nc, nd = c * pa + d * pc, c * pb + d * pd
        scale = 1.0 / na
        a, b, c, d = na * scale, nb * scale, nc * scale, nd * scale
        shift *= 2
    g = a / c
    rho = 1.0 / (g + upp)
    return g, rho, g * rho, place


def fill_tables(width, thick, diff, tab):
    levels = thick.shape[1]
    lane = lax.broadcasted_iota(jnp.int32, (8, levels), 1)
    sub = lax.broadcasted_iota(jnp.int32, (8, levels), 0)
    comps = diff.shape[0]
    rate = jnp.zeros((8, levels), jnp.float32)
    for c in range(comps):
        rate = jnp.where(sub % comps == c, (2.0 * time_step) * diff[c], rate)
    below = jnp.broadcast_to(thick[...], (8, levels))
    above = jnp.where(lane == levels - 1, below, moved(below, -1))
    across = below + above
    low = rate / (across * below)
    upp = rate / (across * above)
    tables = {}
    for sign, first, second in ((1, low, upp), (-1, upp, low)):
        g, rho, ratio, place = pivots(first, second, lane, sign)
        lam = jnp.where(place == 0, 0.0, first * moved(rho, sign))
        window = lam
        for step in range(1, width):
            window = window * moved(lam, sign * step)
        ahead = jnp.where(place == 0, 1.0, moved(ratio, sign))
        tables[sign] = (lam, rho, second * rho, window, g, second, ahead)
    for index in range(QSH + 1):
        tab[index] = jnp.where(sub < comps, tables[1][index], tables[-1][index])
    tab[DT_ACROSS] = time_step / across
    tab[RATE] = rate


def step_kernel(
    rows, cols, group, halves, state, spacing, diffusivity, out, q, thick, diff, vtab, tab, ysend,
    yrecv, wrecv, ploc, dup, tot, be, got, top, ztop, ret, pq, small, ready, sent, load, ysem, wsem,
    s1, s2, s3,
):
    comps, depth, ny, nx = q.shape
    levels = rows * depth
    count = rows // group
    piece = nx // group
    part = ny // halves
    me, col = lax.axis_index("row"), lax.axis_index("col")
    z, g = me // group, me % group
    base = me * depth
    nxt, prv = (col + 1) % cols, (col + cols - 1) % cols
    chunks = [(c, h) for h in range(halves) for c in range(comps)]

    loads = [pltpu.make_async_copy(state, q, load)]
    takes = [
        pltpu.make_async_copy(spacing, thick, small.at[0]),
        pltpu.make_async_copy(diffusivity, diff, small.at[1]),
    ]
    for copy in takes + loads:
        copy.start()

    barrier = pltpu.get_barrier_semaphore()

    def signal(sem, when, device):
        @pl.when(when)
        def _():
            pl.semaphore_signal(sem, inc=1, device_id=device, device_id_type=MESH)

    def greet(device):
        pl.semaphore_signal(barrier, inc=1, device_id=device, device_id_type=MESH)

    def await_ready(o, when):
        @pl.when(when)
        def _():
            pl.semaphore_wait(ready.at[o - 1], 1)

    def peer(o):
        return (g + o) % group

    signal(barrier, me > 0, (jnp.maximum(me - 1, 0), col))
    signal(barrier, me < rows - 1, (jnp.minimum(me + 1, rows - 1), col))
    for o in range(1, group):
        greet((z * group + peer(o), col))
    sides = [nxt] if cols == 2 else [nxt, prv]
    for side in sides:
        greet((me, side))
    for o in range(1, count):
        signal(barrier, z + o < count, (jnp.minimum(z + o, count - 1) * group + g, col))
    greetings = group - 1 + len(sides) + z
    greetings = greetings + jnp.minimum(me, 1) + jnp.minimum(rows - 1 - me, 1)

    pl.semaphore_wait(barrier, greetings)

    def remote(src, dst, kind, sem, device):
        return pltpu.make_async_remote_copy(
            src_ref=src,
            dst_ref=dst,
            send_sem=sent.at[kind],
            recv_sem=sem,
            device_id=device,
            device_id_type=MESH,
        )

    def await_bytes(ref, sem):
        pltpu.make_async_copy(ref, ref, sem).wait()

    def w_down(h):
        here = pl.ds(h * part, part)
        return remote(
            state.at[2, 0, here],
            wrecv.at[1, here],
            W_DOWN,
            wsem.at[1, h],
            (jnp.maximum(me - 1, 0), col),
        )

    def w_up(h):
        here = pl.ds(h * part, part)
        return remote(
            state.at[2, depth - 1, here],
            wrecv.at[0, here],
            W_UP,
            wsem.at[0, h],
            (jnp.minimum(me + 1, rows - 1), col),
        )

    for h in range(halves):

        @pl.when(me > 0)
        def _(h=h):
            w_down(h).start()

        @pl.when(me < rows - 1)
        def _(h=h):
            w_up(h).start()

    for o in range(1, count):
        signal(ready.at[o - 1], z - o >= 0, (jnp.maximum(z - o, 0) * group + g, col))

    for copy in takes:
        copy.wait()
    fill_tables(depth, thick, diff, vtab)
    publish = pltpu.make_async_copy(vtab, tab, small.at[2])
    publish.start()

    def y_copies(c):
        return [
            remote(ysend.at[c, 0], yrecv.at[c, 0], Y_ROWS, ysem, (me, nxt)),
            remote(ysend.at[c, 1], yrecv.at[c, 1], Y_ROWS, ysem, (me, prv)),
        ]

    loads[0].wait()
    for c in range(comps):
        for k in range(depth):
            ysend[c, 0, k : k + 1, :] = q[c, k, ny - 1 : ny, :]
            ysend[c, 1, k : k + 1, :] = q[c, k, 0:1, :]

    for c in range(comps):
        for copy in y_copies(c):
            copy.start()

    @pl.when(me == 0)
    def _():
        wrecv[0] = jnp.zeros((ny, nx), jnp.float32)
        for o in range(1, group):
            pq[:, 2 * o] = jnp.zeros((len(chunks), part, piece), jnp.float32)

    @pl.when(me == rows - 1)
    def _():
        wrecv[1] = jnp.zeros((ny, nx), jnp.float32)
        for o in range(1, group):
            pq[:, 2 * o + 1] = jnp.zeros((len(chunks), part, piece), jnp.float32)

    def up(table, c, level):
        return tab[table, c, jnp.clip(level, 0, levels - 1)]

    def down(table, c, level):
        return tab[table, comps + c, jnp.clip(level, 0, levels - 1)]

    publish.wait()
    slab = 8
    row_of = lax.broadcasted_iota(jnp.int32, (slab, nx), 0)
    half = time_step / (2.0 * cell_width)

    def push(i, o, way=None):
        to = peer(o)
        first, size = (0, 2) if way is None else (way, 1)
        return remote(
            be.at[i, pl.ds(2 * to + first, size)],
            got.at[i, pl.ds(2 * o + first, size)],
            PUSH,
            s1.at[i],
            (z * group + to, col),
        )

    def send_z(i, o, way):
        to = z + o if way == 0 else z - o
        to = jnp.clip(to, 0, count - 1)
        return remote(
            top.at[i, way], ztop.at[i, z_slot(o, way)], ALONG_Z, s2.at[i], (to * group + g, col)
        )

    def z_slot(o, way):
        return count - o - 1 if way == 0 else o - 1

    def give(i, o, way=None):
        to = peer(o)
        first, size = (0, 2) if way is None else (way, 1)
        return remote(
            ret.at[i, pl.ds(2 * to + first, size)],
            pq.at[i, pl.ds(2 * (group - o) + first, size)],
            GIVE,
            s3.at[i],
            (z * group + to, col),
        )

    def start_of(copies, row, outward):
        @pl.when(row == 0)
        def _():
            copies(outward).start()

        @pl.when(row == rows - 1)
        def _():
            copies(1 - outward).start()

        @pl.when((row > 0) & (row < rows - 1))
        def _():
            copies(None).start()

    at_edge = (me == 0) | (me == rows - 1)
    lacking = jnp.where((z == 0) & (g > 0), 1, 0)
    lacking = lacking + jnp.where((z == count - 1) & (g < group - 1), 1, 0)

    def await_edge(refs, sem):
        @pl.when(at_edge)
        def _():
            await_bytes(refs(group - 1), sem)

        @pl.when(jnp.logical_not(at_edge))
        def _():
            await_bytes(refs(2 * (group - 1)), sem)

    def await_lacking(refs, sem):
        for lacks in range(2 if count > 1 else 3):

            @pl.when(lacking == lacks)
            def _(lacks=lacks):
                await_bytes(refs(2 * (group - 1) - lacks), sem)

    def stencil(c):
        alpha = tab[RATE, c, 0] * (0.5 / cell_width**2)
        keep = 1.0 - 4.0 * alpha
        for r in range(0, ny, slab):

            def level(k, carry, c=c, r=r, alpha=alpha, keep=keep):
                below, total, beta = carry
                scale = up(DT_ACROSS, 0, base + k)
                c_up = jnp.where(k == depth - 1, 0.0, scale)
                c_dn = jnp.where(k == 0, 0.0, scale)
                here = pl.ds(r, slab)
                centre = q[c, k, here, :]
                x_left = pltpu.roll(centre, 1, 1)
                x_right = pltpu.roll(centre, nx - 1, 1)
                if r == 0:
                    first = yrecv[c, 0, pl.ds(k, 1), :]
                else:
                    first = q[c, k, r - 1 : r, :]
                if r + slab == ny:
                    last = yrecv[c, 1, pl.ds(k, 1), :]
                else:
                    last = q[c, k, r + slab : r + slab + 1, :]
                y_left = jnp.where(row_of == 0, first, pltpu.roll(centre, 1, 0))
                y_right = jnp.where(row_of == slab - 1, last, pltpu.roll(centre, slab - 1, 0))
                z_up = q[c, jnp.minimum(k + 1, depth - 1), here, :]
                z_dn = q[c, jnp.maximum(k - 1, 0), here, :]
                value = keep * centre + alpha * ((x_left + x_right) + (y_left + y_right))
                value = value - (half * q[0, k, here, :]) * (x_right - x_left)
                value = value - (half * q[1, k, here, :]) * (y_right - y_left)
                value = value - q[2, k, here, :] * (c_up * z_up - c_dn * z_dn)
                if c == 2:
                    value = value + (time_step * buoyancy) * q[3, k, here, :]
                if c == 3:
                    value = value + time_step * q[2, k, here, :]
                below = value + up(LAM, c, base + k) * below
                out[c, k, here, :] = below
                total = total + beta * value
                return below, total, beta * down(LAM, c, base + k)

            start = jnp.zeros((slab, nx), jnp.float32)
            _, total, _ = lax.fori_loop(
                0, depth, level, (start, start, down(LAM, c, base - 1)), unroll=min(depth, UNROLL)
            )
            tot[c, pl.ds(r, slab), :] = total

    def await_w(h):
        @pl.when(me > 0)
        def _():
            w_up(h).wait_recv()

        @pl.when(me < rows - 1)
        def _():
            w_down(h).wait_recv()

    def finish(i):
        c, h = chunks[i]
        beta = down(LAM, c, base - 1)
        for k in range(depth):
            beta = beta * down(LAM, c, base + k)
        pi = 1.0
        for k in range(1, depth):
            pi = pi * up(LAM, c, base + k)
        for r in range(0, part, slab):
            here, local = pl.ds(h * part + r, slab), pl.ds(r, slab)
            below, total = out[c, depth - 1, here, :], tot[c, here, :]
            d_up = up(DT_ACROSS, 0, base + depth) * (wrecv[1, here, :] * q[c, depth - 1, here, :])
            d_dn = -up(DT_ACROSS, 0, base - 1) * (wrecv[0, here, :] * q[c, 0, here, :])
            p_loc = up(LAM, c, base) * d_dn
            ploc[c, here, :] = p_loc
            dup[c, here, :] = down(LAM, c, base + depth - 1) * d_up
            b = up(LAM, c, base + depth) * (below + pi * p_loc) + d_up
            e = total + beta * d_up + d_dn
            for p in range(group):
                be[i, 2 * p, local, :] = b[:, p * piece : (p + 1) * piece]
                be[i, 2 * p + 1, local, :] = e[:, p * piece : (p + 1) * piece]
        for o in range(1, group):
            start_of(functools.partial(push, i, o), me, 0)
        for way in range(2):
            got[i, way] = be[i, 2 * g + way]

    await_bytes(yrecv, ysem)
    for c in range(comps):
        stencil(c)
        if c == min(1, comps - 1):
            await_w(0)
            for i in range(c):
                finish(i)
        if c >= 1:
            finish(c)
    for i in range(comps, len(chunks)):
        if i % comps == 0:
            await_w(i // comps)
        finish(i)

    def up_factor(c, j):
        return up(WIN, c, (j + 1) * depth)

    def down_factor(c, j):
        return down(WIN, c, j * depth - 1)

    def slot(other):
        return (g + group - other) % group

    def gather(i):
        c = chunks[i][0]
        if group > 1:
            await_lacking(lambda size: got.at[i, pl.ds(2, size)], s1.at[i])

        @pl.when(z < count - 1)
        def _():
            total = got[i, 2 * slot(0)]
            for j in range(1, group):
                total = got[i, 2 * slot(j)] + up_factor(c, z * group + j) * total
            top[i, 0] = total

        @pl.when(z > 0)
        def _():
            total = got[i, 2 * slot(group - 1) + 1]
            for j in reversed(range(group - 1)):
                total = got[i, 2 * slot(j) + 1] + down_factor(c, z * group + j) * total
            top[i, 1] = total

        for o in range(1, count):
            if i == 0:
                await_ready(o, z + o < count)

            @pl.when(z + o < count)
            def _(o=o):
                send_z(i, o, 0).start()

            @pl.when(z - o >= 0)
            def _(o=o):
                send_z(i, o, 1).start()

    def scatter(i):
        c = chunks[i][0]
        if count > 1:
            await_bytes(ztop.at[i], s2.at[i])
        for way in range(2):
            acc = ret.at[i, way]
            acc[...] = jnp.zeros((part, piece), jnp.float32)
            weight = 1.0
            for o in range(1, count):
                source = z - o if way == 0 else z + o

                @pl.when((source >= 0) & (source < count))
                def _(o=o, way=way, weight=weight, acc=acc):
                    acc[...] += weight * ztop[i, z_slot(o, way)]

                for j in range(group):
                    device = source * group + j
                    weight = weight * (up_factor if way == 0 else down_factor)(c, device)
        carry = ret[i, 0]
        for j in range(group):
            ret[i, 2 * j] = carry
            if j < group - 1:
                carry = got[i, 2 * slot(j)] + up_factor(c, z * group + j) * carry
        carry = ret[i, 1]
        for j in reversed(range(group)):
            ret[i, 2 * j + 1] = carry
            if j > 0:
                carry = got[i, 2 * slot(j) + 1] + down_factor(c, z * group + j) * carry
        for o in range(1, group):
            start_of(functools.partial(give, i, o), z * group + peer(o), 1)
        for way in range(2):
            pq[i, way] = ret[i, 2 * g + way]

    def settle(i):
        c, h = chunks[i]
        here = pl.ds(h * part, part)
        pis = [jnp.float32(1.0)]
        for k in range(1, depth):
            pis.append(pis[-1] * up(LAM, c, base + k))
        end = base + depth - 1
        den = up(GEE, c, end) + up(UPPER, c, end) * down(QSH, c, end)
        if group > 1:
            await_edge(lambda size: pq.at[i, pl.ds(0, size)], s3.at[i])
        for o in range(group):
            p = peer(o)
            span = pl.ds(pl.multiple_of(p * piece, piece), piece)
            carry = pq[i, 2 * o] + ploc[c, here, span]
            x = out[c, depth - 1, here, span] + pis[-1] * carry
            x = (x + (pq[i, 2 * o + 1] + dup[c, here, span])) / den
            out[c, depth - 1, here, span] = x
            for k in reversed(range(depth - 1)):
                rho = up(RHO, c, base + k)
                x = rho * out[c, k, here, span] + (rho * pis[k]) * carry + up(MU, c, base + k) * x
                out[c, k, here, span] = x

    total_chunks = len(chunks)
    for i in range(total_chunks):
        gather(i)
        if i >= LAG:
            scatter(i - LAG)
    for i in range(max(total_chunks - LAG, 0), total_chunks):
        scatter(i)
    for i in range(total_chunks):
        settle(i)

    await_bytes(ysend, sent.at[Y_ROWS])

    @pl.when(me > 0)
    def _():
        await_bytes(wrecv.at[0], sent.at[W_DOWN])

    @pl.when(me < rows - 1)
    def _():
        await_bytes(wrecv.at[0], sent.at[W_UP])

    if group > 1:
        await_edge(lambda size: be.at[:, pl.ds(0, size)], sent.at[PUSH])
        await_lacking(lambda size: ret.at[:, pl.ds(0, size)], sent.at[GIVE])
    if count > 1:
        await_bytes(ztop, sent.at[ALONG_Z])


def group_of(rows, nx):
    group = 1
    while group * group < rows and rows % (2 * group) == 0 and nx % (256 * group) == 0:
        group *= 2
    return group


def shards(rows, cols, flow_state, spacing, diffusivity):
    comps, depth, ny, nx = flow_state.shape
    group = group_of(rows, nx)
    count = rows // group
    piece = nx // group
    halves = HALVES if ny % (8 * HALVES) == 0 else 1
    part = ny // halves
    chunks = comps * halves
    levels = spacing.shape[0]
    f32 = jnp.float32
    vmem = functools.partial(pltpu.VMEM, dtype=f32)
    dma = pltpu.SemaphoreType.DMA
    spacing = pltpu.with_memory_space_constraint(spacing.reshape(1, levels), pltpu.HBM)
    diffusivity = pltpu.with_memory_space_constraint(diffusivity, pltpu.HBM)
    return pl.pallas_call(
        functools.partial(step_kernel, rows, cols, group, halves),
        out_shape=jax.ShapeDtypeStruct(flow_state.shape, f32),
        in_specs=[pl.BlockSpec(memory_space=pltpu.HBM)] * 3,
        out_specs=pl.BlockSpec(memory_space=pltpu.VMEM),
        scratch_shapes=[
            vmem(flow_state.shape),
            vmem((1, levels)),
            pltpu.SMEM((comps,), f32),
            vmem((TABLES, 8, levels)),
            pltpu.SMEM((TABLES, 8, levels), f32),
            vmem((comps, 2, depth, nx)),
            vmem((comps, 2, depth, nx)),
            vmem((2, ny, nx)),
            vmem((comps, ny, nx)),
            vmem((comps, ny, nx)),
            vmem((comps, ny, nx)),
            vmem((chunks, 2 * group, part, piece)),
            vmem((chunks, 2 * group, part, piece)),
            vmem((chunks, 2, part, piece)),
            vmem((chunks, max(count - 1, 1), part, piece)),
            vmem((chunks, 2 * group, part, piece)),
            vmem((chunks, 2 * group, part, piece)),
            dma((3,)),
            pltpu.SemaphoreType.REGULAR((max(count - 1, 1),)),
            dma((6,)),
            dma,
            dma,
            dma((2, halves)),
            dma((chunks,)),
            dma((chunks,)),
            dma((chunks,)),
        ],
        compiler_params=pltpu.CompilerParams(
            collective_id=0, has_side_effects=True, vmem_limit_bytes=46 << 20
        ),
        name="convection_step",
    )(flow_state, spacing, diffusivity)


def solution(mesh):
    rows, cols = mesh.shape["row"], mesh.shape["col"]
    placed = (P(None, "row", "col", None), P(), P())
    return jax.shard_map(
        functools.partial(shards, rows, cols),
        mesh=mesh,
        in_specs=placed,
        out_specs=P(None, "row", "col", None),
        check_vma=False,
    )
```

```python
import functools

import jax
import jax.numpy as jnp
from jax import lax
from jax.experimental import pallas as pl
from jax.experimental.pallas import tpu as pltpu
from jax.sharding import PartitionSpec as P

time_step = 0.02
cell_width = 0.1
buoyancy = 1.0
UNROLL = 8
HALVES = 2
LAG = 5
MESH = pl.DeviceIdType.MESH

PUSH, ALONG_Z, GIVE, Y_ROWS, W_UP, W_DOWN = range(6)
LAM, RHO, MU, WIN, GEE, UPPER, QSH, DT_ACROSS, RATE, TABLES = range(10)


def moved(value, by):
    return pltpu.roll(value, by % value.shape[1], 1)


def pivots(low, upp, lane, sign):
    levels = low.shape[1]
    place = lane if sign == 1 else levels - 1 - lane
    one, zero = jnp.ones_like(low), jnp.zeros_like(low)
    before = jnp.where(place == 0, one, moved(upp, sign))
    a, b, c, d = one + low, before, one, before
    shift = 1
    while shift < levels:
        inside = place >= shift
        pa = jnp.where(inside, moved(a, sign * shift), one)
        pb = jnp.where(inside, moved(b, sign * shift), zero)
        pc = jnp.where(inside, moved(c, sign * shift), zero)
        pd = jnp.where(inside, moved(d, sign * shift), one)
        na, nb = a * pa + b * pc, a * pb + b * pd
        nc, nd = c * pa + d * pc, c * pb + d * pd
        scale = 1.0 / na
        a, b, c, d = na * scale, nb * scale, nc * scale, nd * scale
        shift *= 2
    g = a / c
    rho = 1.0 / (g + upp)
    return g, rho, g * rho, place


def fill_tables(width, thick, diff, tab):
    levels = thick.shape[1]
    lane = lax.broadcasted_iota(jnp.int32, (8, levels), 1)
    sub = lax.broadcasted_iota(jnp.int32, (8, levels), 0)
    comps = diff.shape[0]
    rate = jnp.zeros((8, levels), jnp.float32)
    for c in range(comps):
        rate = jnp.where(sub % comps == c, (2.0 * time_step) * diff[c], rate)
    below = jnp.broadcast_to(thick[...], (8, levels))
    above = jnp.where(lane == levels - 1, below, moved(below, -1))
    across = below + above
    low = rate / (across * below)
    upp = rate / (across * above)
    tables = {}
    for sign, first, second in ((1, low, upp), (-1, upp, low)):
        g, rho, ratio, place = pivots(first, second, lane, sign)
        lam = jnp.where(place == 0, 0.0, first * moved(rho, sign))
        window = lam
        for step in range(1, width):
            window = window * moved(lam, sign * step)
        ahead = jnp.where(place == 0, 1.0, moved(ratio, sign))
        tables[sign] = (lam, rho, second * rho, window, g, second, ahead)
    for index in range(QSH + 1):
        tab[index] = jnp.where(sub < comps, tables[1][index], tables[-1][index])
    tab[DT_ACROSS] = time_step / across
    tab[RATE] = rate


def step_kernel(
    rows, cols, group, halves, state, spacing, diffusivity, out, q, thick, diff, vtab, tab, ysend,
    yrecv, wrecv, ploc, dup, tot, be, got, top, ztop, ret, pq, small, ready, sent, load, ysem, wsem,
    s1, s2, s3,
):
    comps, depth, ny, nx = q.shape
    levels = rows * depth
    count = rows // group
    piece = nx // group
    part = ny // halves
    me, col = lax.axis_index("row"), lax.axis_index("col")
    z, g = me // group, me % group
    base = me * depth
    nxt, prv = (col + 1) % cols, (col + cols - 1) % cols
    chunks = [(c, h) for h in range(halves) for c in range(comps)]

    loads = [pltpu.make_async_copy(state, q, load)]
    takes = [
        pltpu.make_async_copy(spacing, thick, small.at[0]),
        pltpu.make_async_copy(diffusivity, diff, small.at[1]),
    ]
    for copy in takes + loads:
        copy.start()

    barrier = pltpu.get_barrier_semaphore()

    def signal(sem, when, device):
        @pl.when(when)
        def _():
            pl.semaphore_signal(sem, inc=1, device_id=device, device_id_type=MESH)

    def greet(device):
        pl.semaphore_signal(barrier, inc=1, device_id=device, device_id_type=MESH)

    def await_ready(index, when):
        @pl.when(when)
        def _():
            pl.semaphore_wait(ready.at[index], 1)

    def peer(o):
        return (g + o) % group

    even = g % 2 == 0
    last = g == group - 1

    def twin(o):
        return jnp.where(even, o == 1, o == group - 1)

    if group > 1:
        greet((z * group + g + jnp.where(even, 1, -1), col))
    sides = [nxt] if cols == 2 else [nxt, prv]
    for side in sides:
        greet((me, side))
    for o in range(1, group):
        signal(barrier, (g + o < group) & ~twin(o), (z * group + peer(o), col))
    for o in range(1, count):
        signal(barrier, z + o < count, (jnp.minimum(z + o, count - 1) * group + g, col))
    greetings = len(sides) + z
    if group > 1:
        greetings = greetings + g + jnp.where(even, 1, 0)
    pl.semaphore_wait(barrier, greetings)

    along_z = group - 1
    for o in range(1, count):
        signal(ready.at[along_z + o], z - o >= 0, (jnp.maximum(z - o, 0) * group + g, col))
    for o in range(1, group):
        signal(ready.at[group - o], (g + o >= group) & ~twin(o), (z * group + peer(o), col))

    def remote(src, dst, kind, sem, device):
        return pltpu.make_async_remote_copy(
            src_ref=src,
            dst_ref=dst,
            send_sem=sent.at[kind],
            recv_sem=sem,
            device_id=device,
            device_id_type=MESH,
        )

    def await_bytes(ref, sem):
        pltpu.make_async_copy(ref, ref, sem).wait()

    def w_down(h):
        here = pl.ds(h * part, part)
        return remote(
            state.at[2, 0, here],
            wrecv.at[1, here],
            W_DOWN,
            wsem.at[1, h],
            (jnp.maximum(me - 1, 0), col),
        )

    def w_up(h):
        here = pl.ds(h * part, part)
        return remote(
            state.at[2, depth - 1, here],
            wrecv.at[0, here],
            W_UP,
            wsem.at[0, h],
            (jnp.minimum(me + 1, rows - 1), col),
        )

    def send_w(way, when):
        @pl.when(when & ((me < rows - 1) if way else (me > 0)))
        def _():
            for h in range(halves):
                (w_up if way else w_down)(h).start()

    send_w(0, g > 0)
    send_w(1, even & ~last)

    for copy in takes:
        copy.wait()
    fill_tables(depth, thick, diff, vtab)
    publish = pltpu.make_async_copy(vtab, tab, small.at[2])
    publish.start()

    if group > 1:
        await_ready(1, ~even & ~last)
        await_ready(group - 1, (g == 0) & (z > 0) & ~twin(group - 1))
    if count > 1:
        await_ready(along_z + 1, last & (z < count - 1))
    send_w(1, ~even | last)
    send_w(0, g == 0)

    def y_copies(c):
        return [
            remote(ysend.at[c, 0], yrecv.at[c, 0], Y_ROWS, ysem, (me, nxt)),
            remote(ysend.at[c, 1], yrecv.at[c, 1], Y_ROWS, ysem, (me, prv)),
        ]

    loads[0].wait()
    for c in range(comps):
        for k in range(depth):
            ysend[c, 0, k : k + 1, :] = q[c, k, ny - 1 : ny, :]
            ysend[c, 1, k : k + 1, :] = q[c, k, 0:1, :]

    for c in range(comps):
        for copy in y_copies(c):
            copy.start()

    @pl.when(me == 0)
    def _():
        wrecv[0] = jnp.zeros((ny, nx), jnp.float32)
        for o in range(1, group):
            pq[:, 2 * o] = jnp.zeros((len(chunks), part, piece), jnp.float32)

    @pl.when(me == rows - 1)
    def _():
        wrecv[1] = jnp.zeros((ny, nx), jnp.float32)
        for o in range(1, group):
            pq[:, 2 * o + 1] = jnp.zeros((len(chunks), part, piece), jnp.float32)

    def up(table, c, level):
        return tab[table, c, jnp.clip(level, 0, levels - 1)]

    def down(table, c, level):
        return tab[table, comps + c, jnp.clip(level, 0, levels - 1)]

    publish.wait()
    slab = 8
    row_of = lax.broadcasted_iota(jnp.int32, (slab, nx), 0)
    half = time_step / (2.0 * cell_width)

    def push(i, o, way=None):
        to = peer(o)
        first, size = (0, 2) if way is None else (way, 1)
        return remote(
            be.at[i, pl.ds(2 * to + first, size)],
            got.at[i, pl.ds(2 * o + first, size)],
            PUSH,
            s1.at[i],
            (z * group + to, col),
        )

    def send_z(i, o, way):
        to = z + o if way == 0 else z - o
        to = jnp.clip(to, 0, count - 1)
        return remote(
            top.at[i, way], ztop.at[i, z_slot(o, way)], ALONG_Z, s2.at[i], (to * group + g, col)
        )

    def z_slot(o, way):
        return count - o - 1 if way == 0 else o - 1

    def give(i, to, way=None):
        first, size = (0, 2) if way is None else (way, 1)
        return remote(
            ret.at[i, pl.ds(2 * to + first, size)],
            pq.at[i, pl.ds(2 * slot(to) + first, size)],
            GIVE,
            s3.at[i],
            (z * group + to, col),
        )

    def start_of(copies, row, outward):
        @pl.when(row == 0)
        def _():
            copies(outward).start()

        @pl.when(row == rows - 1)
        def _():
            copies(1 - outward).start()

        @pl.when((row > 0) & (row < rows - 1))
        def _():
            copies(None).start()

    at_edge = (me == 0) | (me == rows - 1)
    lacking = jnp.where((z == 0) & (g > 0), 1, 0)
    lacking = lacking + jnp.where((z == count - 1) & (g < group - 1), 1, 0)

    def await_edge(refs, sem):
        @pl.when(at_edge)
        def _():
            await_bytes(refs(group - 1), sem)

        @pl.when(jnp.logical_not(at_edge))
        def _():
            await_bytes(refs(2 * (group - 1)), sem)

    def await_lacking(refs, sem):
        for lacks in range(2 if count > 1 else 3):

            @pl.when(lacking == lacks)
            def _(lacks=lacks):
                await_bytes(refs(2 * (group - 1) - lacks), sem)

    def stencil(c):
        alpha = tab[RATE, c, 0] * (0.5 / cell_width**2)
        keep = 1.0 - 4.0 * alpha
        for r in range(0, ny, slab):

            def level(k, carry, c=c, r=r, alpha=alpha, keep=keep):
                below, total, beta = carry
                scale = up(DT_ACROSS, 0, base + k)
                c_up = jnp.where(k == depth - 1, 0.0, scale)
                c_dn = jnp.where(k == 0, 0.0, scale)
                here = pl.ds(r, slab)
                centre = q[c, k, here, :]
                x_left = pltpu.roll(centre, 1, 1)
                x_right = pltpu.roll(centre, nx - 1, 1)
                if r == 0:
                    first = yrecv[c, 0, pl.ds(k, 1), :]
                else:
                    first = q[c, k, r - 1 : r, :]
                if r + slab == ny:
                    last = yrecv[c, 1, pl.ds(k, 1), :]
                else:
                    last = q[c, k, r + slab : r + slab + 1, :]
                y_left = jnp.where(row_of == 0, first, pltpu.roll(centre, 1, 0))
                y_right = jnp.where(row_of == slab - 1, last, pltpu.roll(centre, slab - 1, 0))
                z_up = q[c, jnp.minimum(k + 1, depth - 1), here, :]
                z_dn = q[c, jnp.maximum(k - 1, 0), here, :]
                value = keep * centre + alpha * ((x_left + x_right) + (y_left + y_right))
                value = value - (half * q[0, k, here, :]) * (x_right - x_left)
                value = value - (half * q[1, k, here, :]) * (y_right - y_left)
                value = value - q[2, k, here, :] * (c_up * z_up - c_dn * z_dn)
                if c == 2:
                    value = value + (time_step * buoyancy) * q[3, k, here, :]
                if c == 3:
                    value = value + time_step * q[2, k, here, :]
                below = value + up(LAM, c, base + k) * below
                out[c, k, here, :] = below
                total = total + beta * value
                return below, total, beta * down(LAM, c, base + k)

            start = jnp.zeros((slab, nx), jnp.float32)
            _, total, _ = lax.fori_loop(
                0, depth, level, (start, start, down(LAM, c, base - 1)), unroll=min(depth, UNROLL)
            )
            tot[c, pl.ds(r, slab), :] = total

    def await_w(h):
        @pl.when(me > 0)
        def _():
            w_up(h).wait_recv()

        @pl.when(me < rows - 1)
        def _():
            w_down(h).wait_recv()

    def finish(i):
        c, h = chunks[i]
        beta = down(LAM, c, base - 1)
        for k in range(depth):
            beta = beta * down(LAM, c, base + k)
        pi = 1.0
        for k in range(1, depth):
            pi = pi * up(LAM, c, base + k)
        for r in range(0, part, slab):
            here, local = pl.ds(h * part + r, slab), pl.ds(r, slab)
            below, total = out[c, depth - 1, here, :], tot[c, here, :]
            d_up = up(DT_ACROSS, 0, base + depth) * (wrecv[1, here, :] * q[c, depth - 1, here, :])
            d_dn = -up(DT_ACROSS, 0, base - 1) * (wrecv[0, here, :] * q[c, 0, here, :])
            p_loc = up(LAM, c, base) * d_dn
            ploc[c, here, :] = p_loc
            dup[c, here, :] = down(LAM, c, base + depth - 1) * d_up
            b = up(LAM, c, base + depth) * (below + pi * p_loc) + d_up
            e = total + beta * d_up + d_dn
            for p in range(group):
                be[i, 2 * p, local, :] = b[:, p * piece : (p + 1) * piece]
                be[i, 2 * p + 1, local, :] = e[:, p * piece : (p + 1) * piece]
        for o in range(1, group):
            if i == 0:
                heard = ((o == 1) & ~even) | ((o == group - 1) & (g == 0) & (z > 0))
                await_ready(o, (g + o < group) & ~twin(o) & ~heard)
            start_of(functools.partial(push, i, o), me, 0)
        for way in range(2):
            got[i, way] = be[i, 2 * g + way]

    await_bytes(yrecv, ysem)
    for c in range(comps):
        stencil(c)
        if c == min(1, comps - 1):
            await_w(0)
            for i in range(c):
                finish(i)
        if c >= 1:
            finish(c)
    for i in range(comps, len(chunks)):
        if i % comps == 0:
            await_w(i // comps)
        finish(i)

    def up_factor(c, j):
        return up(WIN, c, (j + 1) * depth)

    def down_factor(c, j):
        return down(WIN, c, j * depth - 1)

    def slot(other):
        return (g + group - other) % group

    def gather(i):
        c = chunks[i][0]
        if group > 1:
            await_lacking(lambda size: got.at[i, pl.ds(2, size)], s1.at[i])

        if i == 0:
            for o in range(1, count):
                await_ready(along_z + o, (z + o < count) & ~(last & (o == 1)))

        @pl.when(z > 0)
        def _():
            total = got[i, 2 * slot(group - 1) + 1]
            for j in reversed(range(group - 1)):
                total = got[i, 2 * slot(j) + 1] + down_factor(c, z * group + j) * total
            top[i, 1] = total

        for o in reversed(range(1, count)):

            @pl.when(z - o >= 0)
            def _(o=o):
                send_z(i, o, 1).start()

        @pl.when(z < count - 1)
        def _():
            total = got[i, 2 * slot(0)]
            for j in range(1, group):
                total = got[i, 2 * slot(j)] + up_factor(c, z * group + j) * total
            top[i, 0] = total

        for o in reversed(range(1, count)):

            @pl.when(z + o < count)
            def _(o=o):
                send_z(i, o, 0).start()

    def scatter(i):
        c = chunks[i][0]
        if count > 1:
            await_bytes(ztop.at[i], s2.at[i])
        for way in range(2):
            acc = ret.at[i, way]
            acc[...] = jnp.zeros((part, piece), jnp.float32)
            weight = 1.0
            for o in range(1, count):
                source = z - o if way == 0 else z + o

                @pl.when((source >= 0) & (source < count))
                def _(o=o, way=way, weight=weight, acc=acc):
                    acc[...] += weight * ztop[i, z_slot(o, way)]

                for j in range(group):
                    device = source * group + j
                    weight = weight * (up_factor if way == 0 else down_factor)(c, device)
        carry = ret[i, 0]
        for j in range(group):
            ret[i, 2 * j] = carry
            if j < group - 1:
                carry = got[i, 2 * slot(j)] + up_factor(c, z * group + j) * carry
        carry = ret[i, 1]
        for j in reversed(range(group)):
            ret[i, 2 * j + 1] = carry
            if j > 0:
                carry = got[i, 2 * slot(j) + 1] + down_factor(c, z * group + j) * carry
        for to in range(group):

            @pl.when(g != to)
            def _(to=to):
                start_of(functools.partial(give, i, to), z * group + to, 1)

        for way in range(2):
            pq[i, way] = ret[i, 2 * g + way]

    def settle(i):
        c, h = chunks[i]
        here = pl.ds(h * part, part)
        pis = [jnp.float32(1.0)]
        for k in range(1, depth):
            pis.append(pis[-1] * up(LAM, c, base + k))
        end = base + depth - 1
        den = up(GEE, c, end) + up(UPPER, c, end) * down(QSH, c, end)
        if group > 1:
            await_edge(lambda size: pq.at[i, pl.ds(0, size)], s3.at[i])
        for o in range(group):
            p = peer(o)
            span = pl.ds(pl.multiple_of(p * piece, piece), piece)
            carry = pq[i, 2 * o] + ploc[c, here, span]
            x = out[c, depth - 1, here, span] + pis[-1] * carry
            x = (x + (pq[i, 2 * o + 1] + dup[c, here, span])) / den
            out[c, depth - 1, here, span] = x
            for k in reversed(range(depth - 1)):
                rho = up(RHO, c, base + k)
                x = rho * out[c, k, here, span] + (rho * pis[k]) * carry + up(MU, c, base + k) * x
                out[c, k, here, span] = x

    total_chunks = len(chunks)
    for i in range(total_chunks):
        gather(i)
        if i >= LAG:
            scatter(i - LAG)
    for i in range(max(total_chunks - LAG, 0), total_chunks):
        scatter(i)
    for i in range(total_chunks):
        settle(i)

    await_bytes(ysend, sent.at[Y_ROWS])

    @pl.when(me > 0)
    def _():
        await_bytes(wrecv.at[0], sent.at[W_DOWN])

    @pl.when(me < rows - 1)
    def _():
        await_bytes(wrecv.at[0], sent.at[W_UP])

    if group > 1:
        await_edge(lambda size: be.at[:, pl.ds(0, size)], sent.at[PUSH])
        await_lacking(lambda size: ret.at[:, pl.ds(0, size)], sent.at[GIVE])
    if count > 1:
        await_bytes(ztop, sent.at[ALONG_Z])


def group_of(rows, nx):
    group = 1
    while group * group < rows and rows % (2 * group) == 0 and nx % (256 * group) == 0:
        group *= 2
    return group


def shards(rows, cols, flow_state, spacing, diffusivity):
    comps, depth, ny, nx = flow_state.shape
    group = group_of(rows, nx)
    count = rows // group
    piece = nx // group
    halves = HALVES if ny % (8 * HALVES) == 0 else 1
    part = ny // halves
    chunks = comps * halves
    levels = spacing.shape[0]
    f32 = jnp.float32
    vmem = functools.partial(pltpu.VMEM, dtype=f32)
    dma = pltpu.SemaphoreType.DMA
    spacing = pltpu.with_memory_space_constraint(spacing.reshape(1, levels), pltpu.HBM)
    diffusivity = pltpu.with_memory_space_constraint(diffusivity, pltpu.HBM)
    return pl.pallas_call(
        functools.partial(step_kernel, rows, cols, group, halves),
        out_shape=jax.ShapeDtypeStruct(flow_state.shape, f32),
        in_specs=[pl.BlockSpec(memory_space=pltpu.HBM)] * 3,
        out_specs=pl.BlockSpec(memory_space=pltpu.VMEM),
        scratch_shapes=[
            vmem(flow_state.shape),
            vmem((1, levels)),
            pltpu.SMEM((comps,), f32),
            vmem((TABLES, 8, levels)),
            pltpu.SMEM((TABLES, 8, levels), f32),
            vmem((comps, 2, depth, nx)),
            vmem((comps, 2, depth, nx)),
            vmem((2, ny, nx)),
            vmem((comps, ny, nx)),
            vmem((comps, ny, nx)),
            vmem((comps, ny, nx)),
            vmem((chunks, 2 * group, part, piece)),
            vmem((chunks, 2 * group, part, piece)),
            vmem((chunks, 2, part, piece)),
            vmem((chunks, max(count - 1, 1), part, piece)),
            vmem((chunks, 2 * group, part, piece)),
            vmem((chunks, 2 * group, part, piece)),
            dma((3,)),
            pltpu.SemaphoreType.REGULAR((group + count,)),
            dma((6,)),
            dma,
            dma,
            dma((2, halves)),
            dma((chunks,)),
            dma((chunks,)),
            dma((chunks,)),
        ],
        compiler_params=pltpu.CompilerParams(
            collective_id=0, has_side_effects=True, vmem_limit_bytes=46 << 20
        ),
        name="convection_step",
    )(flow_state, spacing, diffusivity)


def solution(mesh):
    rows, cols = mesh.shape["row"], mesh.shape["col"]
    placed = (P(None, "row", "col", None), P(), P())
    return jax.shard_map(
        functools.partial(shards, rows, cols),
        mesh=mesh,
        in_specs=placed,
        out_specs=P(None, "row", "col", None),
        check_vma=False,
    )
```

```python
import functools

import jax
import jax.numpy as jnp
from jax import lax
from jax.experimental import pallas as pl
from jax.experimental.pallas import tpu as pltpu
from jax.sharding import PartitionSpec as P

time_step = 0.02
cell_width = 0.1
buoyancy = 1.0
UNROLL = 8
HALVES = 2
LAG = 5
MESH = pl.DeviceIdType.MESH

PUSH, ALONG_Z, GIVE, Y_ROWS, W_UP, W_DOWN = range(6)
LAM, RHO, MU, WIN, GEE, UPPER, QSH, DT_ACROSS, RATE, TABLES = range(10)


def moved(value, by):
    return pltpu.roll(value, by % value.shape[1], 1)


def pivots(low, upp, lane, sign):
    levels = low.shape[1]
    place = lane if sign == 1 else levels - 1 - lane
    one, zero = jnp.ones_like(low), jnp.zeros_like(low)
    before = jnp.where(place == 0, one, moved(upp, sign))
    a, b, c, d = one + low, before, one, before
    shift = 1
    while shift < levels:
        inside = place >= shift
        pa = jnp.where(inside, moved(a, sign * shift), one)
        pb = jnp.where(inside, moved(b, sign * shift), zero)
        pc = jnp.where(inside, moved(c, sign * shift), zero)
        pd = jnp.where(inside, moved(d, sign * shift), one)
        na, nb = a * pa + b * pc, a * pb + b * pd
        nc, nd = c * pa + d * pc, c * pb + d * pd
        scale = 1.0 / na
        a, b, c, d = na * scale, nb * scale, nc * scale, nd * scale
        shift *= 2
    g = a / c
    rho = 1.0 / (g + upp)
    return g, rho, g * rho, place


def fill_tables(width, thick, diff, tab):
    levels = thick.shape[1]
    lane = lax.broadcasted_iota(jnp.int32, (8, levels), 1)
    sub = lax.broadcasted_iota(jnp.int32, (8, levels), 0)
    comps = diff.shape[0]
    rate = jnp.zeros((8, levels), jnp.float32)
    for c in range(comps):
        rate = jnp.where(sub % comps == c, (2.0 * time_step) * diff[c], rate)
    below = jnp.broadcast_to(thick[...], (8, levels))
    above = jnp.where(lane == levels - 1, below, moved(below, -1))
    across = below + above
    low = rate / (across * below)
    upp = rate / (across * above)
    tables = {}
    for sign, first, second in ((1, low, upp), (-1, upp, low)):
        g, rho, ratio, place = pivots(first, second, lane, sign)
        lam = jnp.where(place == 0, 0.0, first * moved(rho, sign))
        window = lam
        for step in range(1, width):
            window = window * moved(lam, sign * step)
        ahead = jnp.where(place == 0, 1.0, moved(ratio, sign))
        tables[sign] = (lam, rho, second * rho, window, g, second, ahead)
    for index in range(QSH + 1):
        tab[index] = jnp.where(sub < comps, tables[1][index], tables[-1][index])
    tab[DT_ACROSS] = time_step / across
    tab[RATE] = rate


def step_kernel(
    rows, cols, group, halves, state, spacing, diffusivity, out, q, thick, diff, vtab, tab, ysend,
    yrecv, wrecv, ploc, dup, tot, be, got, top, ztop, ret, pq, small, ready, sent, load, ysem, wsem,
    s1, s2, s3,
):
    comps, depth, ny, nx = q.shape
    levels = rows * depth
    count = rows // group
    piece = nx // group
    part = ny // halves
    me, col = lax.axis_index("row"), lax.axis_index("col")
    z, g = me // group, me % group
    base = me * depth
    nxt, prv = (col + 1) % cols, (col + cols - 1) % cols
    chunks = [(c, h) for h in range(halves) for c in range(comps)]

    loads = [pltpu.make_async_copy(state, q, load)]
    takes = [
        pltpu.make_async_copy(spacing, thick, small.at[0]),
        pltpu.make_async_copy(diffusivity, diff, small.at[1]),
    ]
    barrier = pltpu.get_barrier_semaphore()

    def signal(sem, when, device):
        @pl.when(when)
        def _():
            pl.semaphore_signal(sem, inc=1, device_id=device, device_id_type=MESH)

    def greet(device):
        pl.semaphore_signal(barrier, inc=1, device_id=device, device_id_type=MESH)

    def await_ready(index, when):
        @pl.when(when)
        def _():
            pl.semaphore_wait(ready.at[index], 1)

    def peer(o):
        return (g + o) % group

    even = g % 2 == 0
    last = g == group - 1

    def twin(o):
        return jnp.where(even, o == 1, o == group - 1)

    if group > 1:
        greet((z * group + g + jnp.where(even, 1, -1), col))
    sides = [nxt] if cols == 2 else [nxt, prv]
    for side in sides:
        greet((me, side))
    for o in range(1, group):
        signal(barrier, (g + o < group) & ~twin(o), (z * group + peer(o), col))
    for o in range(1, count):
        signal(barrier, z + o < count, (jnp.minimum(z + o, count - 1) * group + g, col))
    for copy in takes + loads:
        copy.start()

    greetings = len(sides) + z
    if group > 1:
        greetings = greetings + g + jnp.where(even, 1, 0)
    pl.semaphore_wait(barrier, greetings)

    along_z = group - 1
    for o in range(1, count):
        signal(ready.at[along_z + o], z - o >= 0, (jnp.maximum(z - o, 0) * group + g, col))
    for o in range(1, group):
        signal(ready.at[group - o], (g + o >= group) & ~twin(o), (z * group + peer(o), col))

    def remote(src, dst, kind, sem, device):
        return pltpu.make_async_remote_copy(
            src_ref=src,
            dst_ref=dst,
            send_sem=sent.at[kind],
            recv_sem=sem,
            device_id=device,
            device_id_type=MESH,
        )

    def await_bytes(ref, sem):
        pltpu.make_async_copy(ref, ref, sem).wait()

    def w_down(h):
        here = pl.ds(h * part, part)
        return remote(
            state.at[2, 0, here],
            wrecv.at[1, here],
            W_DOWN,
            wsem.at[1, h],
            (jnp.maximum(me - 1, 0), col),
        )

    def w_up(h):
        here = pl.ds(h * part, part)
        return remote(
            state.at[2, depth - 1, here],
            wrecv.at[0, here],
            W_UP,
            wsem.at[0, h],
            (jnp.minimum(me + 1, rows - 1), col),
        )

    def send_w(way, when):
        @pl.when(when & ((me < rows - 1) if way else (me > 0)))
        def _():
            for h in range(halves):
                (w_up if way else w_down)(h).start()

    send_w(0, g > 0)
    send_w(1, even & ~last)

    for copy in takes:
        copy.wait()
    fill_tables(depth, thick, diff, vtab)
    publish = pltpu.make_async_copy(vtab, tab, small.at[2])
    publish.start()

    if group > 1:
        await_ready(1, ~even & ~last)
        await_ready(group - 1, (g == 0) & (z > 0) & ~twin(group - 1))
    if count > 1:
        await_ready(along_z + 1, last & (z < count - 1))
    send_w(1, ~even | last)
    send_w(0, g == 0)

    def y_copies(c):
        return [
            remote(ysend.at[c, 0], yrecv.at[c, 0], Y_ROWS, ysem, (me, nxt)),
            remote(ysend.at[c, 1], yrecv.at[c, 1], Y_ROWS, ysem, (me, prv)),
        ]

    loads[0].wait()
    for c in range(comps):
        for k in range(depth):
            ysend[c, 0, k : k + 1, :] = q[c, k, ny - 1 : ny, :]
            ysend[c, 1, k : k + 1, :] = q[c, k, 0:1, :]

    for c in range(comps):
        for copy in y_copies(c):
            copy.start()

    @pl.when(me == 0)
    def _():
        wrecv[0] = jnp.zeros((ny, nx), jnp.float32)
        for o in range(1, group):
            pq[:, 2 * o] = jnp.zeros((len(chunks), part, piece), jnp.float32)

    @pl.when(me == rows - 1)
    def _():
        wrecv[1] = jnp.zeros((ny, nx), jnp.float32)
        for o in range(1, group):
            pq[:, 2 * o + 1] = jnp.zeros((len(chunks), part, piece), jnp.float32)

    def up(table, c, level):
        return tab[table, c, jnp.clip(level, 0, levels - 1)]

    def down(table, c, level):
        return tab[table, comps + c, jnp.clip(level, 0, levels - 1)]

    publish.wait()
    slab = 8
    row_of = lax.broadcasted_iota(jnp.int32, (slab, nx), 0)
    half = time_step / (2.0 * cell_width)

    def push(i, o, way=None):
        to = peer(o)
        first, size = (0, 2) if way is None else (way, 1)
        return remote(
            be.at[i, pl.ds(2 * to + first, size)],
            got.at[i, pl.ds(2 * o + first, size)],
            PUSH,
            s1.at[i],
            (z * group + to, col),
        )

    def send_z(i, o, way):
        to = z + o if way == 0 else z - o
        to = jnp.clip(to, 0, count - 1)
        return remote(
            top.at[i, way], ztop.at[i, z_slot(o, way)], ALONG_Z, s2.at[i], (to * group + g, col)
        )

    def z_slot(o, way):
        return count - o - 1 if way == 0 else o - 1

    def give(i, to, way=None):
        first, size = (0, 2) if way is None else (way, 1)
        return remote(
            ret.at[i, pl.ds(2 * to + first, size)],
            pq.at[i, pl.ds(2 * slot(to) + first, size)],
            GIVE,
            s3.at[i if i < len(chunks) - 1 else i + slot(to) - 1],
            (z * group + to, col),
        )

    def start_of(copies, row, outward):
        @pl.when(row == 0)
        def _():
            copies(outward).start()

        @pl.when(row == rows - 1)
        def _():
            copies(1 - outward).start()

        @pl.when((row > 0) & (row < rows - 1))
        def _():
            copies(None).start()

    at_edge = (me == 0) | (me == rows - 1)
    lacking = jnp.where((z == 0) & (g > 0), 1, 0)
    lacking = lacking + jnp.where((z == count - 1) & (g < group - 1), 1, 0)

    def await_edge(refs, sem, partners):
        @pl.when(at_edge)
        def _():
            await_bytes(refs(partners), sem)

        @pl.when(jnp.logical_not(at_edge))
        def _():
            await_bytes(refs(2 * partners), sem)

    def await_lacking(refs, sem):
        for lacks in range(2 if count > 1 else 3):

            @pl.when(lacking == lacks)
            def _(lacks=lacks):
                await_bytes(refs(2 * (group - 1) - lacks), sem)

    def stencil(c):
        alpha = tab[RATE, c, 0] * (0.5 / cell_width**2)
        keep = 1.0 - 4.0 * alpha
        for r in range(0, ny, slab):

            def level(k, carry, c=c, r=r, alpha=alpha, keep=keep):
                below, total, beta = carry
                scale = up(DT_ACROSS, 0, base + k)
                c_up = jnp.where(k == depth - 1, 0.0, scale)
                c_dn = jnp.where(k == 0, 0.0, scale)
                here = pl.ds(r, slab)
                centre = q[c, k, here, :]
                x_left = pltpu.roll(centre, 1, 1)
                x_right = pltpu.roll(centre, nx - 1, 1)
                if r == 0:
                    first = yrecv[c, 0, pl.ds(k, 1), :]
                else:
                    first = q[c, k, r - 1 : r, :]
                if r + slab == ny:
                    last = yrecv[c, 1, pl.ds(k, 1), :]
                else:
                    last = q[c, k, r + slab : r + slab + 1, :]
                y_left = jnp.where(row_of == 0, first, pltpu.roll(centre, 1, 0))
                y_right = jnp.where(row_of == slab - 1, last, pltpu.roll(centre, slab - 1, 0))
                z_up = q[c, jnp.minimum(k + 1, depth - 1), here, :]
                z_dn = q[c, jnp.maximum(k - 1, 0), here, :]
                value = keep * centre + alpha * ((x_left + x_right) + (y_left + y_right))
                value = value - (half * q[0, k, here, :]) * (x_right - x_left)
                value = value - (half * q[1, k, here, :]) * (y_right - y_left)
                value = value - q[2, k, here, :] * (c_up * z_up - c_dn * z_dn)
                if c == 2:
                    value = value + (time_step * buoyancy) * q[3, k, here, :]
                if c == 3:
                    value = value + time_step * q[2, k, here, :]
                below = value + up(LAM, c, base + k) * below
                out[c, k, here, :] = below
                total = total + beta * value
                return below, total, beta * down(LAM, c, base + k)

            start = jnp.zeros((slab, nx), jnp.float32)
            _, total, _ = lax.fori_loop(
                0, depth, level, (start, start, down(LAM, c, base - 1)), unroll=min(depth, UNROLL)
            )
            tot[c, pl.ds(r, slab), :] = total

    def await_w(h):
        @pl.when(me > 0)
        def _():
            w_up(h).wait_recv()

        @pl.when(me < rows - 1)
        def _():
            w_down(h).wait_recv()

    def finish(i):
        c, h = chunks[i]
        beta = down(LAM, c, base - 1)
        for k in range(depth):
            beta = beta * down(LAM, c, base + k)
        pi = 1.0
        for k in range(1, depth):
            pi = pi * up(LAM, c, base + k)
        for r in range(0, part, slab):
            here, local = pl.ds(h * part + r, slab), pl.ds(r, slab)
            below, total = out[c, depth - 1, here, :], tot[c, here, :]
            d_up = up(DT_ACROSS, 0, base + depth) * (wrecv[1, here, :] * q[c, depth - 1, here, :])
            d_dn = -up(DT_ACROSS, 0, base - 1) * (wrecv[0, here, :] * q[c, 0, here, :])
            p_loc = up(LAM, c, base) * d_dn
            ploc[c, here, :] = p_loc
            dup[c, here, :] = down(LAM, c, base + depth - 1) * d_up
            b = up(LAM, c, base + depth) * (below + pi * p_loc) + d_up
            e = total + beta * d_up + d_dn
            for p in range(group):
                be[i, 2 * p, local, :] = b[:, p * piece : (p + 1) * piece]
                be[i, 2 * p + 1, local, :] = e[:, p * piece : (p + 1) * piece]
        for o in range(1, group):
            if i == 0:
                heard = ((o == 1) & ~even) | ((o == group - 1) & (g == 0) & (z > 0))
                await_ready(o, (g + o < group) & ~twin(o) & ~heard)
            start_of(functools.partial(push, i, o), me, 0)
        for way in range(2):
            got[i, way] = be[i, 2 * g + way]

    await_bytes(yrecv, ysem)
    for c in range(comps):
        stencil(c)
        if c == min(1, comps - 1):
            await_w(0)
            for i in range(c):
                finish(i)
        if c >= 1:
            finish(c)
    for i in range(comps, len(chunks)):
        if i % comps == 0:
            await_w(i // comps)
        finish(i)

    def up_factor(c, j):
        return up(WIN, c, (j + 1) * depth)

    def down_factor(c, j):
        return down(WIN, c, j * depth - 1)

    def slot(other):
        return (g + group - other) % group

    def gather(i):
        c = chunks[i][0]
        if group > 1:
            await_lacking(lambda size: got.at[i, pl.ds(2, size)], s1.at[i])

        if i == 0:
            for o in range(1, count):
                await_ready(along_z + o, (z + o < count) & ~(last & (o == 1)))

        @pl.when(z > 0)
        def _():
            total = got[i, 2 * slot(group - 1) + 1]
            for j in reversed(range(group - 1)):
                total = got[i, 2 * slot(j) + 1] + down_factor(c, z * group + j) * total
            top[i, 1] = total

        for o in reversed(range(1, count)):

            @pl.when(z - o >= 0)
            def _(o=o):
                send_z(i, o, 1).start()

        @pl.when(z < count - 1)
        def _():
            total = got[i, 2 * slot(0)]
            for j in range(1, group):
                total = got[i, 2 * slot(j)] + up_factor(c, z * group + j) * total
            top[i, 0] = total

        for o in reversed(range(1, count)):

            @pl.when(z + o < count)
            def _(o=o):
                send_z(i, o, 0).start()

    def scatter(i):
        c = chunks[i][0]
        if count > 1:
            await_bytes(ztop.at[i], s2.at[i])
        for way in range(2):
            acc = ret.at[i, way]
            acc[...] = jnp.zeros((part, piece), jnp.float32)
            weight = 1.0
            for o in range(1, count):
                source = z - o if way == 0 else z + o

                @pl.when((source >= 0) & (source < count))
                def _(o=o, way=way, weight=weight, acc=acc):
                    acc[...] += weight * ztop[i, z_slot(o, way)]

                for j in range(group):
                    device = source * group + j
                    weight = weight * (up_factor if way == 0 else down_factor)(c, device)
        carry = ret[i, 0]
        for j in range(group):
            ret[i, 2 * j] = carry
            if j < group - 1:
                carry = got[i, 2 * slot(j)] + up_factor(c, z * group + j) * carry
        carry = ret[i, 1]
        for j in reversed(range(group)):
            ret[i, 2 * j + 1] = carry
            if j > 0:
                carry = got[i, 2 * slot(j) + 1] + down_factor(c, z * group + j) * carry
        for to in range(group):

            @pl.when(g != to)
            def _(to=to):
                start_of(functools.partial(give, i, to), z * group + to, 1)

        for way in range(2):
            pq[i, way] = ret[i, 2 * g + way]

    def settle(i):
        c, h = chunks[i]
        here = pl.ds(h * part, part)
        pis = [jnp.float32(1.0)]
        for k in range(1, depth):
            pis.append(pis[-1] * up(LAM, c, base + k))
        end = base + depth - 1
        den = up(GEE, c, end) + up(UPPER, c, end) * down(QSH, c, end)
        final = i == len(chunks) - 1
        if group > 1 and not final:
            await_edge(lambda size: pq.at[i, pl.ds(0, size)], s3.at[i], group - 1)
        for o in sorted(range(group), key=lambda o: (o > 0, o % 2)):
            p = peer(o)
            if o and final:
                await_edge(lambda size: pq.at[i, pl.ds(2 * o, size)], s3.at[i + o - 1], 1)
            span = pl.ds(pl.multiple_of(p * piece, piece), piece)
            carry = pq[i, 2 * o] + ploc[c, here, span]
            x = out[c, depth - 1, here, span] + pis[-1] * carry
            x = (x + (pq[i, 2 * o + 1] + dup[c, here, span])) / den
            out[c, depth - 1, here, span] = x
            for k in reversed(range(depth - 1)):
                rho = up(RHO, c, base + k)
                x = rho * out[c, k, here, span] + (rho * pis[k]) * carry + up(MU, c, base + k) * x
                out[c, k, here, span] = x

    total_chunks = len(chunks)
    for i in range(total_chunks):
        gather(i)
        if i >= LAG:
            scatter(i - LAG)
    settled = 0
    for i in range(max(total_chunks - LAG, 0), total_chunks):
        scatter(i)
        if i >= total_chunks - 2:
            settle(settled)
            settled += 1
    for i in range(settled, total_chunks):
        settle(i)

    await_bytes(ysend, sent.at[Y_ROWS])

    @pl.when(me > 0)
    def _():
        await_bytes(wrecv.at[0], sent.at[W_DOWN])

    @pl.when(me < rows - 1)
    def _():
        await_bytes(wrecv.at[0], sent.at[W_UP])

    if group > 1:
        await_edge(lambda size: be.at[:, pl.ds(0, size)], sent.at[PUSH], group - 1)
        await_lacking(lambda size: ret.at[:, pl.ds(0, size)], sent.at[GIVE])
    if count > 1:
        await_bytes(ztop, sent.at[ALONG_Z])


def group_of(rows, nx):
    group = 1
    while group * group < rows and rows % (2 * group) == 0 and nx % (256 * group) == 0:
        group *= 2
    return group


def shards(rows, cols, flow_state, spacing, diffusivity):
    comps, depth, ny, nx = flow_state.shape
    group = group_of(rows, nx)
    count = rows // group
    piece = nx // group
    halves = HALVES if ny % (8 * HALVES) == 0 else 1
    part = ny // halves
    chunks = comps * halves
    levels = spacing.shape[0]
    f32 = jnp.float32
    vmem = functools.partial(pltpu.VMEM, dtype=f32)
    dma = pltpu.SemaphoreType.DMA
    spacing = pltpu.with_memory_space_constraint(spacing.reshape(1, levels), pltpu.HBM)
    diffusivity = pltpu.with_memory_space_constraint(diffusivity, pltpu.HBM)
    return pl.pallas_call(
        functools.partial(step_kernel, rows, cols, group, halves),
        out_shape=jax.ShapeDtypeStruct(flow_state.shape, f32),
        in_specs=[pl.BlockSpec(memory_space=pltpu.HBM)] * 3,
        out_specs=pl.BlockSpec(memory_space=pltpu.VMEM),
        scratch_shapes=[
            vmem(flow_state.shape),
            vmem((1, levels)),
            pltpu.SMEM((comps,), f32),
            vmem((TABLES, 8, levels)),
            pltpu.SMEM((TABLES, 8, levels), f32),
            vmem((comps, 2, depth, nx)),
            vmem((comps, 2, depth, nx)),
            vmem((2, ny, nx)),
            vmem((comps, ny, nx)),
            vmem((comps, ny, nx)),
            vmem((comps, ny, nx)),
            vmem((chunks, 2 * group, part, piece)),
            vmem((chunks, 2 * group, part, piece)),
            vmem((chunks, 2, part, piece)),
            vmem((chunks, max(count - 1, 1), part, piece)),
            vmem((chunks, 2 * group, part, piece)),
            vmem((chunks, 2 * group, part, piece)),
            dma((3,)),
            pltpu.SemaphoreType.REGULAR((max(group + count - 1, 1),)),
            dma((6,)),
            dma,
            dma,
            dma((2, halves)),
            dma((chunks,)),
            dma((chunks,)),
            dma((chunks - 1 + max(group - 1, 1),)),
        ],
        compiler_params=pltpu.CompilerParams(
            collective_id=0, has_side_effects=True, vmem_limit_bytes=46 << 20
        ),
        name="convection_step",
    )(flow_state, spacing, diffusivity)


def solution(mesh):
    rows, cols = mesh.shape["row"], mesh.shape["col"]
    placed = (P(None, "row", "col", None), P(), P())
    return jax.shard_map(
        functools.partial(shards, rows, cols),
        mesh=mesh,
        in_specs=placed,
        out_specs=P(None, "row", "col", None),
        check_vma=False,
    )
```

```python
import functools

import jax
import jax.numpy as jnp
from jax import lax
from jax.experimental import pallas as pl
from jax.experimental.pallas import tpu as pltpu
from jax.sharding import PartitionSpec as P

time_step = 0.02
cell_width = 0.1
buoyancy = 1.0
UNROLL = 8
HALVES = 2
LAG = 5
MESH = pl.DeviceIdType.MESH

PUSH, ALONG_Z, GIVE, Y_ROWS, W_UP, W_DOWN = range(6)
LAM, RHO, MU, WIN, GEE, UPPER, QSH, DT_ACROSS, RATE, TABLES = range(10)


def moved(value, by):
    return pltpu.roll(value, by % value.shape[1], 1)


def pivots(low, upp, lane, sign):
    levels = low.shape[1]
    place = lane if sign == 1 else levels - 1 - lane
    one, zero = jnp.ones_like(low), jnp.zeros_like(low)
    before = jnp.where(place == 0, one, moved(upp, sign))
    a, b, c, d = one + low, before, one, before
    shift = 1
    while shift < levels:
        inside = place >= shift
        pa = jnp.where(inside, moved(a, sign * shift), one)
        pb = jnp.where(inside, moved(b, sign * shift), zero)
        pc = jnp.where(inside, moved(c, sign * shift), zero)
        pd = jnp.where(inside, moved(d, sign * shift), one)
        na, nb = a * pa + b * pc, a * pb + b * pd
        nc, nd = c * pa + d * pc, c * pb + d * pd
        scale = 1.0 / na
        a, b, c, d = na * scale, nb * scale, nc * scale, nd * scale
        shift *= 2
    g = a / c
    rho = 1.0 / (g + upp)
    return g, rho, g * rho, place


def fill_tables(width, thick, diff, tab):
    levels = thick.shape[1]
    lane = lax.broadcasted_iota(jnp.int32, (8, levels), 1)
    sub = lax.broadcasted_iota(jnp.int32, (8, levels), 0)
    comps = diff.shape[0]
    rate = jnp.zeros((8, levels), jnp.float32)
    for c in range(comps):
        rate = jnp.where(sub % comps == c, (2.0 * time_step) * diff[c], rate)
    below = jnp.broadcast_to(thick[...], (8, levels))
    above = jnp.where(lane == levels - 1, below, moved(below, -1))
    across = below + above
    low = rate / (across * below)
    upp = rate / (across * above)
    tables = {}
    for sign, first, second in ((1, low, upp), (-1, upp, low)):
        g, rho, ratio, place = pivots(first, second, lane, sign)
        lam = jnp.where(place == 0, 0.0, first * moved(rho, sign))
        window = lam
        for step in range(1, width):
            window = window * moved(lam, sign * step)
        ahead = jnp.where(place == 0, 1.0, moved(ratio, sign))
        tables[sign] = (lam, rho, second * rho, window, g, second, ahead)
    for index in range(QSH + 1):
        tab[index] = jnp.where(sub < comps, tables[1][index], tables[-1][index])
    tab[DT_ACROSS] = time_step / across
    tab[RATE] = rate


def step_kernel(
    rows, cols, group, halves, state, spacing, diffusivity, out, q, thick, diff, vtab, tab, ysend,
    yrecv, wrecv, ploc, dup, tot, be, got, top, ztop, ret, pq, small, ready, sent, load, ysem, wsem,
    s1, s2, s3,
):
    comps, depth, ny, nx = q.shape
    levels = rows * depth
    count = rows // group
    piece = nx // group
    part = ny // halves
    me, col = lax.axis_index("row"), lax.axis_index("col")
    z, g = me // group, me % group
    base = me * depth
    nxt, prv = (col + 1) % cols, (col + cols - 1) % cols
    chunks = [(c, h) for h in range(halves) for c in range(comps)]

    loads = [pltpu.make_async_copy(state, q, load)]
    takes = [
        pltpu.make_async_copy(spacing, thick, small.at[0]),
        pltpu.make_async_copy(diffusivity, diff, small.at[1]),
    ]
    barrier = pltpu.get_barrier_semaphore()

    def signal(sem, when, device):
        @pl.when(when)
        def _():
            pl.semaphore_signal(sem, inc=1, device_id=device, device_id_type=MESH)

    def greet(device):
        pl.semaphore_signal(barrier, inc=1, device_id=device, device_id_type=MESH)

    def await_ready(index, when):
        @pl.when(when)
        def _():
            pl.semaphore_wait(ready.at[index], 1)

    def peer(o):
        return (g + o) % group

    even = g % 2 == 0
    last = g == group - 1

    def twin(o):
        return jnp.where(even, o == 1, o == group - 1)

    if group > 1:
        greet((z * group + g + jnp.where(even, 1, -1), col))
    sides = [nxt] if cols == 2 else [nxt, prv]
    for side in sides:
        greet((me, side))
    for o in range(1, group):
        signal(barrier, (g + o < group) & ~twin(o), (z * group + peer(o), col))
    for o in range(1, count):
        signal(barrier, z + o < count, (jnp.minimum(z + o, count - 1) * group + g, col))
    for copy in takes + loads:
        copy.start()

    greetings = len(sides) + z
    if group > 1:
        greetings = greetings + g + jnp.where(even, 1, 0)
    pl.semaphore_wait(barrier, greetings)

    along_z = group - 1
    for o in range(1, count):
        signal(ready.at[along_z + o], z - o >= 0, (jnp.maximum(z - o, 0) * group + g, col))
    for o in range(1, group):
        signal(ready.at[group - o], (g + o >= group) & ~twin(o), (z * group + peer(o), col))

    def remote(src, dst, kind, sem, device):
        return pltpu.make_async_remote_copy(
            src_ref=src,
            dst_ref=dst,
            send_sem=sent.at[kind],
            recv_sem=sem,
            device_id=device,
            device_id_type=MESH,
        )

    def await_bytes(ref, sem):
        pltpu.make_async_copy(ref, ref, sem).wait()

    def w_down(h):
        here = pl.ds(h * part, part)
        return remote(
            state.at[2, 0, here],
            wrecv.at[1, here],
            W_DOWN,
            wsem.at[1, h],
            (jnp.maximum(me - 1, 0), col),
        )

    def w_up(h):
        here = pl.ds(h * part, part)
        return remote(
            state.at[2, depth - 1, here],
            wrecv.at[0, here],
            W_UP,
            wsem.at[0, h],
            (jnp.minimum(me + 1, rows - 1), col),
        )

    def send_w(way, when):
        @pl.when(when & ((me < rows - 1) if way else (me > 0)))
        def _():
            for h in range(halves):
                (w_up if way else w_down)(h).start()

    send_w(0, g > 0)
    send_w(1, even & ~last)

    if group > 1:
        await_ready(1, ~even & ~last)
        await_ready(group - 1, (g == 0) & (z > 0) & ~twin(group - 1))
    if count > 1:
        await_ready(along_z + 1, last & (z < count - 1))
    send_w(1, ~even | last)
    send_w(0, g == 0)

    def y_copies(c):
        return [
            remote(ysend.at[c, 0], yrecv.at[c, 0], Y_ROWS, ysem, (me, nxt)),
            remote(ysend.at[c, 1], yrecv.at[c, 1], Y_ROWS, ysem, (me, prv)),
        ]

    loads[0].wait()
    for c in range(comps):
        for k in range(depth):
            ysend[c, 0, k : k + 1, :] = q[c, k, ny - 1 : ny, :]
            ysend[c, 1, k : k + 1, :] = q[c, k, 0:1, :]

    for c in range(comps):
        for copy in y_copies(c):
            copy.start()

    for copy in takes:
        copy.wait()
    fill_tables(depth, thick, diff, vtab)
    publish = pltpu.make_async_copy(vtab, tab, small.at[2])
    publish.start()

    @pl.when(me == 0)
    def _():
        wrecv[0] = jnp.zeros((ny, nx), jnp.float32)
        for o in range(1, group):
            pq[:, 2 * o] = jnp.zeros((len(chunks), part, piece), jnp.float32)

    @pl.when(me == rows - 1)
    def _():
        wrecv[1] = jnp.zeros((ny, nx), jnp.float32)
        for o in range(1, group):
            pq[:, 2 * o + 1] = jnp.zeros((len(chunks), part, piece), jnp.float32)

    def up(table, c, level):
        return tab[table, c, jnp.clip(level, 0, levels - 1)]

    def down(table, c, level):
        return tab[table, comps + c, jnp.clip(level, 0, levels - 1)]

    publish.wait()
    slab = 8
    row_of = lax.broadcasted_iota(jnp.int32, (slab, nx), 0)
    half = time_step / (2.0 * cell_width)

    def push(i, o, way=None):
        to = peer(o)
        first, size = (0, 2) if way is None else (way, 1)
        return remote(
            be.at[i, pl.ds(2 * to + first, size)],
            got.at[i, pl.ds(2 * o + first, size)],
            PUSH,
            s1.at[i],
            (z * group + to, col),
        )

    def send_z(i, o, way):
        to = z + o if way == 0 else z - o
        to = jnp.clip(to, 0, count - 1)
        return remote(
            top.at[i, way], ztop.at[i, z_slot(o, way)], ALONG_Z, s2.at[i], (to * group + g, col)
        )

    def z_slot(o, way):
        return count - o - 1 if way == 0 else o - 1

    def give(i, to, way=None):
        first, size = (0, 2) if way is None else (way, 1)
        return remote(
            ret.at[i, pl.ds(2 * to + first, size)],
            pq.at[i, pl.ds(2 * slot(to) + first, size)],
            GIVE,
            s3.at[i if i < len(chunks) - 1 else i + slot(to) - 1],
            (z * group + to, col),
        )

    def start_of(copies, row, outward):
        @pl.when(row == 0)
        def _():
            copies(outward).start()

        @pl.when(row == rows - 1)
        def _():
            copies(1 - outward).start()

        @pl.when((row > 0) & (row < rows - 1))
        def _():
            copies(None).start()

    at_edge = (me == 0) | (me == rows - 1)
    lacking = jnp.where((z == 0) & (g > 0), 1, 0)
    lacking = lacking + jnp.where((z == count - 1) & (g < group - 1), 1, 0)

    def await_edge(refs, sem, partners):
        @pl.when(at_edge)
        def _():
            await_bytes(refs(partners), sem)

        @pl.when(jnp.logical_not(at_edge))
        def _():
            await_bytes(refs(2 * partners), sem)

    def await_lacking(refs, sem):
        for lacks in range(2 if count > 1 else 3):

            @pl.when(lacking == lacks)
            def _(lacks=lacks):
                await_bytes(refs(2 * (group - 1) - lacks), sem)

    def stencil(c):
        alpha = tab[RATE, c, 0] * (0.5 / cell_width**2)
        keep = 1.0 - 4.0 * alpha
        for r in range(0, ny, slab):

            def level(k, carry, c=c, r=r, alpha=alpha, keep=keep):
                below, total, beta = carry
                scale = up(DT_ACROSS, 0, base + k)
                c_up = jnp.where(k == depth - 1, 0.0, scale)
                c_dn = jnp.where(k == 0, 0.0, scale)
                here = pl.ds(r, slab)
                centre = q[c, k, here, :]
                x_left = pltpu.roll(centre, 1, 1)
                x_right = pltpu.roll(centre, nx - 1, 1)
                if r == 0:
                    first = yrecv[c, 0, pl.ds(k, 1), :]
                else:
                    first = q[c, k, r - 1 : r, :]
                if r + slab == ny:
                    last = yrecv[c, 1, pl.ds(k, 1), :]
                else:
                    last = q[c, k, r + slab : r + slab + 1, :]
                y_left = jnp.where(row_of == 0, first, pltpu.roll(centre, 1, 0))
                y_right = jnp.where(row_of == slab - 1, last, pltpu.roll(centre, slab - 1, 0))
                z_up = q[c, jnp.minimum(k + 1, depth - 1), here, :]
                z_dn = q[c, jnp.maximum(k - 1, 0), here, :]
                value = keep * centre + alpha * ((x_left + x_right) + (y_left + y_right))
                value = value - (half * q[0, k, here, :]) * (x_right - x_left)
                value = value - (half * q[1, k, here, :]) * (y_right - y_left)
                value = value - q[2, k, here, :] * (c_up * z_up - c_dn * z_dn)
                if c == 2:
                    value = value + (time_step * buoyancy) * q[3, k, here, :]
                if c == 3:
                    value = value + time_step * q[2, k, here, :]
                below = value + up(LAM, c, base + k) * below
                out[c, k, here, :] = below
                total = total + beta * value
                return below, total, beta * down(LAM, c, base + k)

            start = jnp.zeros((slab, nx), jnp.float32)
            _, total, _ = lax.fori_loop(
                0, depth, level, (start, start, down(LAM, c, base - 1)), unroll=min(depth, UNROLL)
            )
            tot[c, pl.ds(r, slab), :] = total

    def await_w(h):
        @pl.when(me > 0)
        def _():
            w_up(h).wait_recv()

        @pl.when(me < rows - 1)
        def _():
            w_down(h).wait_recv()

    def finish(i):
        c, h = chunks[i]
        beta = down(LAM, c, base - 1)
        for k in range(depth):
            beta = beta * down(LAM, c, base + k)
        pi = 1.0
        for k in range(1, depth):
            pi = pi * up(LAM, c, base + k)
        for r in range(0, part, slab):
            here, local = pl.ds(h * part + r, slab), pl.ds(r, slab)
            below, total = out[c, depth - 1, here, :], tot[c, here, :]
            d_up = up(DT_ACROSS, 0, base + depth) * (wrecv[1, here, :] * q[c, depth - 1, here, :])
            d_dn = -up(DT_ACROSS, 0, base - 1) * (wrecv[0, here, :] * q[c, 0, here, :])
            p_loc = up(LAM, c, base) * d_dn
            ploc[c, here, :] = p_loc
            dup[c, here, :] = down(LAM, c, base + depth - 1) * d_up
            b = up(LAM, c, base + depth) * (below + pi * p_loc) + d_up
            e = total + beta * d_up + d_dn
            for p in range(group):
                be[i, 2 * p, local, :] = b[:, p * piece : (p + 1) * piece]
                be[i, 2 * p + 1, local, :] = e[:, p * piece : (p + 1) * piece]
        for o in range(1, group):
            if i == 0:
                heard = ((o == 1) & ~even) | ((o == group - 1) & (g == 0) & (z > 0))
                await_ready(o, (g + o < group) & ~twin(o) & ~heard)
            start_of(functools.partial(push, i, o), me, 0)
        for way in range(2):
            got[i, way] = be[i, 2 * g + way]

    await_bytes(yrecv, ysem)
    for c in range(comps):
        stencil(c)
        if c == min(1, comps - 1):
            await_w(0)
            for i in range(c):
                finish(i)
        if c >= 1:
            finish(c)
    for i in range(comps, len(chunks)):
        if i % comps == 0:
            await_w(i // comps)
        finish(i)

    def up_factor(c, j):
        return up(WIN, c, (j + 1) * depth)

    def down_factor(c, j):
        return down(WIN, c, j * depth - 1)

    def slot(other):
        return (g + group - other) % group

    def gather(i):
        c = chunks[i][0]
        if group > 1:
            await_lacking(lambda size: got.at[i, pl.ds(2, size)], s1.at[i])

        if i == 0:
            for o in range(1, count):
                await_ready(along_z + o, (z + o < count) & ~(last & (o == 1)))

        @pl.when(z > 0)
        def _():
            total = got[i, 2 * slot(group - 1) + 1]
            for j in reversed(range(group - 1)):
                total = got[i, 2 * slot(j) + 1] + down_factor(c, z * group + j) * total
            top[i, 1] = total

        for o in reversed(range(1, count)):

            @pl.when(z - o >= 0)
            def _(o=o):
                send_z(i, o, 1).start()

        @pl.when(z < count - 1)
        def _():
            total = got[i, 2 * slot(0)]
            for j in range(1, group):
                total = got[i, 2 * slot(j)] + up_factor(c, z * group + j) * total
            top[i, 0] = total

        for o in reversed(range(1, count)):

            @pl.when(z + o < count)
            def _(o=o):
                send_z(i, o, 0).start()

    def scatter(i):
        c = chunks[i][0]
        if count > 1:
            await_bytes(ztop.at[i], s2.at[i])
        for way in range(2):
            acc = ret.at[i, way]
            acc[...] = jnp.zeros((part, piece), jnp.float32)
            weight = 1.0
            for o in range(1, count):
                source = z - o if way == 0 else z + o

                @pl.when((source >= 0) & (source < count))
                def _(o=o, way=way, weight=weight, acc=acc):
                    acc[...] += weight * ztop[i, z_slot(o, way)]

                for j in range(group):
                    device = source * group + j
                    weight = weight * (up_factor if way == 0 else down_factor)(c, device)
        carry = ret[i, 0]
        for j in range(group):
            ret[i, 2 * j] = carry
            if j < group - 1:
                carry = got[i, 2 * slot(j)] + up_factor(c, z * group + j) * carry
        carry = ret[i, 1]
        for j in reversed(range(group)):
            ret[i, 2 * j + 1] = carry
            if j > 0:
                carry = got[i, 2 * slot(j) + 1] + down_factor(c, z * group + j) * carry
        for to in range(group):

            @pl.when(g != to)
            def _(to=to):
                start_of(functools.partial(give, i, to), z * group + to, 1)

        for way in range(2):
            pq[i, way] = ret[i, 2 * g + way]

    def settle(i):
        c, h = chunks[i]
        here = pl.ds(h * part, part)
        pis = [jnp.float32(1.0)]
        for k in range(1, depth):
            pis.append(pis[-1] * up(LAM, c, base + k))
        end = base + depth - 1
        den = up(GEE, c, end) + up(UPPER, c, end) * down(QSH, c, end)
        final = i == len(chunks) - 1
        if group > 1 and not final:
            await_edge(lambda size: pq.at[i, pl.ds(0, size)], s3.at[i], group - 1)
        for o in sorted(range(group), key=lambda o: (o > 0, o % 2)):
            p = peer(o)
            if o and final:
                await_edge(lambda size: pq.at[i, pl.ds(2 * o, size)], s3.at[i + o - 1], 1)
            span = pl.ds(pl.multiple_of(p * piece, piece), piece)
            carry = pq[i, 2 * o] + ploc[c, here, span]
            x = out[c, depth - 1, here, span] + pis[-1] * carry
            x = (x + (pq[i, 2 * o + 1] + dup[c, here, span])) / den
            out[c, depth - 1, here, span] = x
            for k in reversed(range(depth - 1)):
                rho = up(RHO, c, base + k)
                x = rho * out[c, k, here, span] + (rho * pis[k]) * carry + up(MU, c, base + k) * x
                out[c, k, here, span] = x

    total_chunks = len(chunks)
    for i in range(total_chunks):
        gather(i)
        if i >= LAG:
            scatter(i - LAG)
    settled = 0
    for i in range(max(total_chunks - LAG, 0), total_chunks):
        scatter(i)
        if i >= total_chunks - 2:
            settle(settled)
            settled += 1
    for i in range(settled, total_chunks):
        settle(i)

    await_bytes(ysend, sent.at[Y_ROWS])

    @pl.when(me > 0)
    def _():
        await_bytes(wrecv.at[0], sent.at[W_DOWN])

    @pl.when(me < rows - 1)
    def _():
        await_bytes(wrecv.at[0], sent.at[W_UP])

    if group > 1:
        await_edge(lambda size: be.at[:, pl.ds(0, size)], sent.at[PUSH], group - 1)
        await_lacking(lambda size: ret.at[:, pl.ds(0, size)], sent.at[GIVE])
    if count > 1:
        await_bytes(ztop, sent.at[ALONG_Z])


def group_of(rows, nx):
    group = 1
    while group * group < rows and rows % (2 * group) == 0 and nx % (256 * group) == 0:
        group *= 2
    return group


def shards(rows, cols, flow_state, spacing, diffusivity):
    comps, depth, ny, nx = flow_state.shape
    group = group_of(rows, nx)
    count = rows // group
    piece = nx // group
    halves = HALVES if ny % (8 * HALVES) == 0 else 1
    part = ny // halves
    chunks = comps * halves
    levels = spacing.shape[0]
    f32 = jnp.float32
    vmem = functools.partial(pltpu.VMEM, dtype=f32)
    dma = pltpu.SemaphoreType.DMA
    spacing = pltpu.with_memory_space_constraint(spacing.reshape(1, levels), pltpu.HBM)
    diffusivity = pltpu.with_memory_space_constraint(diffusivity, pltpu.HBM)
    return pl.pallas_call(
        functools.partial(step_kernel, rows, cols, group, halves),
        out_shape=jax.ShapeDtypeStruct(flow_state.shape, f32),
        in_specs=[pl.BlockSpec(memory_space=pltpu.HBM)] * 3,
        out_specs=pl.BlockSpec(memory_space=pltpu.VMEM),
        scratch_shapes=[
            vmem(flow_state.shape),
            vmem((1, levels)),
            pltpu.SMEM((comps,), f32),
            vmem((TABLES, 8, levels)),
            pltpu.SMEM((TABLES, 8, levels), f32),
            vmem((comps, 2, depth, nx)),
            vmem((comps, 2, depth, nx)),
            vmem((2, ny, nx)),
            vmem((comps, ny, nx)),
            vmem((comps, ny, nx)),
            vmem((comps, ny, nx)),
            vmem((chunks, 2 * group, part, piece)),
            vmem((chunks, 2 * group, part, piece)),
            vmem((chunks, 2, part, piece)),
            vmem((chunks, max(count - 1, 1), part, piece)),
            vmem((chunks, 2 * group, part, piece)),
            vmem((chunks, 2 * group, part, piece)),
            dma((3,)),
            pltpu.SemaphoreType.REGULAR((max(group + count - 1, 1),)),
            dma((6,)),
            dma,
            dma,
            dma((2, halves)),
            dma((chunks,)),
            dma((chunks,)),
            dma((chunks - 1 + max(group - 1, 1),)),
        ],
        compiler_params=pltpu.CompilerParams(
            collective_id=0, has_side_effects=True, vmem_limit_bytes=46 << 20
        ),
        name="convection_step",
    )(flow_state, spacing, diffusivity)


def solution(mesh):
    rows, cols = mesh.shape["row"], mesh.shape["col"]
    placed = (P(None, "row", "col", None), P(), P())
    return jax.shard_map(
        functools.partial(shards, rows, cols),
        mesh=mesh,
        in_specs=placed,
        out_specs=P(None, "row", "col", None),
        check_vma=False,
    )
```
